768 devices in a mesh: grp: 2 (over z_hi), row: 48 (over x, z_lo, core), col: 8 (over y).
Axes of the slice: x: 4, y: 8, z: 12 (z_hi: 2, z_lo: 6; z = z_hi * 6 + z_lo), core: 2. Of those that a mesh axis runs over, the one named last changes fastest.
Arguments:
- right_side: float32 [2, 16, 147456], P(None, None, 'row'), may hold values from -6 to 6
- near_tiles: bfloat16 [2, 6144, 256, 256], P(None, ('grp', 'row', 'col')), may hold values from -0.078125 to 0.078125
- tile_pairs: int32 [6144], P(('grp', 'row', 'col')), may hold values from 0 to 59, as said below
- tile_count: int32 [768], P(('grp', 'row', 'col')), may hold values from 1 to 8, as said below
- panel_expansions: bfloat16 [2, 147456, 441], P(None, 'row'), may hold values from -0.125 to 0.125
- leaf_of_panel: int32 [48, 3072], P('row'), may hold values from 0 to 23, never falling along the last dimension, each value on 1 to 256 neighbouring positions
- far_pick: int32 [48, 48, 2], replicated, may hold values from 0 to 23, as said below
- far_target: int32 [48, 96], P('row'), may hold values from 0 to 23
- far_offset: int32 [48, 96], P('row'), may hold values from 0 to 3
- translations: bfloat16 [4, 2, 441, 441], replicated, may hold values from -0.109375 to 0.109375
Outputs:
- solution: float32 [2, 16, 147456], P(None, None, 'row')
The draws below stay inside these ranges and needn't reach their ends.
Inputs may be any that keep to these rules, and one draw needn't show every extreme that they name: `tile_pairs`: within one device's 8 slots the codes are distinct, and over the live slots of all devices with the same row index they are distinct too. `tile_count`: some device has all 8 slots live. far_pick[d, r] holds 2 distinct leaves.
All inputs are finite; a program needn't handle non-finite values.
Results may differ from the reference program's by a relative error of at most 0.0016.
Values may be sent and summed in bfloat16 or wider, within the bound.
A program may use at most 64 MiB of HBM per device.

```python
import math
import jax
import jax.numpy as jnp
import numpy as np
from jax import lax

TILE = 256
COEFS = 441
FIELDS = 16
BLK_DEV = 12
REACH = 2
SLOT_DEV = 8
SEND = 2
OFFSETS = 4
LEAF_DEV = 24
PAN_DEV = 3072
PANELS = 147456
BLOCKS = 576
TILES = 6144
ITEMS = 96
N_GRP = 2
N_ROW = 48
N_COL = 8


def live_counts(key):
    device_count = N_GRP * N_ROW * N_COL
    group_count = N_GRP * N_COL
    code_count = BLK_DEV * (2 * REACH + 1)
    upper = min(SLOT_DEV, (code_count - SLOT_DEV) // (group_count - 1))
    counts = jax.random.randint(jax.random.fold_in(key, 11), (device_count,), 1, upper + 1)
    busiest = jax.random.randint(jax.random.fold_in(key, 12), (), 0, device_count)
    counts = jnp.where(jnp.arange(device_count) == busiest, SLOT_DEV, counts)
    return counts.astype(jnp.int32)


def draw_tile_count(key, part):
    return live_counts(key)


def draw_tile_pairs(key, part):
    group_count = N_GRP * N_COL
    code_count = BLK_DEV * (2 * REACH + 1)
    counts = live_counts(key).reshape(N_GRP, N_ROW, N_COL).transpose(1, 0, 2).reshape(N_ROW, group_count)
    starts = jnp.cumsum(counts, axis=1) - counts
    row_keys = jax.random.split(jax.random.fold_in(key, 13), N_ROW)

    def one_row(row_key):
        return jax.random.permutation(row_key, code_count)
    orders = jax.vmap(one_row)(row_keys)
    positions = (starts[:, :, None] + jnp.arange(SLOT_DEV, dtype=jnp.int32)[None, None, :]) % code_count
    codes = jnp.take_along_axis(orders, positions.reshape(N_ROW, -1), axis=1)
    codes = codes.reshape(N_ROW, N_GRP, N_COL, SLOT_DEV).transpose(1, 0, 2, 3)
    return codes.reshape(-1).astype(jnp.int32)


def draw_far_pick(key, part):
    pair_keys = jax.random.split(key, N_ROW * N_ROW)

    def one_pair(pair_key):
        return jax.random.permutation(pair_key, LEAF_DEV)[:SEND]
    return jax.vmap(one_pair)(pair_keys).reshape(N_ROW, N_ROW, SEND).astype(jnp.int32)


def plant(drawn, stream_key, low, high):
    spot = [jax.random.randint(jax.random.fold_in(stream_key, axis), (), 0, length) for axis, length in enumerate(drawn.shape)]
    main_axis = drawn.shape.index(max(drawn.shape))
    next_to = spot[:main_axis] + [(spot[main_axis] + 1) % drawn.shape[main_axis]] + spot[main_axis + 1:]
    return drawn.at[tuple(spot)].set(low).at[tuple(next_to)].set(high)


def block_scale(stream_key, shape, shards, smallest, top_value):
    level, own = 1.0, jax.random.fold_in(stream_key, 6)
    for dim, blocks in shards:
        heights = jnp.exp(jax.random.uniform(jax.random.fold_in(own, dim), (blocks,), jnp.float32, smallest / len(shards), top_value / len(shards)))
        level = level * jnp.repeat(heights, shape[dim] // blocks).reshape([-1 if axis == dim else 1 for axis in range(len(shape))])
    return level


def profile(count, total, reach, lean):
    portions = [(1 << 20) // math.isqrt(standing ** lean) + 1 for standing in range(2, count + 1)]
    spare, holding = total - reach - (count - 1), [1] * (count - 1)
    while spare > 0:
        free = [i for i in range(count - 1) if holding[i] < reach]
        mass, remaining = sum([portions[i] for i in free]), spare
        for i in free:
            addition = min(reach - holding[i], max(1, remaining * portions[i] // mass), spare)
            holding[i] = holding[i] + addition
            spare = spare - addition
    return np.array([reach] + holding)


def ragged(key, count, total, reach, slope):
    if count == 2:
        one = jax.random.randint(key, (), max(1, total - reach), min(reach, total - 1) + 1)
        return jnp.stack([one, total - one])
    lengths = jnp.asarray(profile(count, total, reach, slope), jnp.int32)
    couples = (count - 1) // 2
    donor, receiver = lengths[1:1 + 2 * couples:2], lengths[2:2 + 2 * couples:2]
    margin = jnp.minimum(donor - 1, reach - receiver)
    passed = jax.random.randint(jax.random.fold_in(key, 1), (couples,), 0, 1 << 20) % (margin + 1)
    lengths = lengths.at[1:1 + 2 * couples:2].set(donor - passed).at[2:2 + 2 * couples:2].set(receiver + passed)
    return lengths[jax.random.permutation(jax.random.fold_in(key, 2), count)]


def scatter_about(own_key, shape, deviation, reach, cuts=(), held_as=jnp.bfloat16):
    drawn = deviation * jax.random.normal(own_key, shape, jnp.float32)
    if cuts:
        drawn = drawn * block_scale(own_key, shape, cuts, -0.22, 0.18)
    return jnp.clip(drawn, -reach, reach).astype(held_as)


def setup_inputs(seed: int = 0) -> dict:
    seeds = jax.random.split(jax.random.key(seed), 11)
    right_side = scatter_about(seeds[0], (2, FIELDS, PANELS), 1.0, 6.0, ((2, 48),), jnp.float32)
    near_tiles = scatter_about(seeds[1], (2, TILES, TILE, TILE), (4 * TILE * (2 * REACH + 1)) ** -0.5, 0.078125, ((1, 768),))
    tile_pairs = draw_tile_pairs(jax.random.fold_in(seeds[10], 71), 0)
    tile_count = draw_tile_count(jax.random.fold_in(seeds[10], 71), 0)
    panel_expansions = scatter_about(seeds[4], (2, PANELS, COEFS), (4 * COEFS) ** -0.5, 0.125, ((1, 48),))
    leaf_of_panel = jax.vmap(lambda own: jnp.searchsorted(jnp.cumsum(ragged(own, LEAF_DEV, PAN_DEV, 2 * PAN_DEV // LEAF_DEV, 1)), jnp.arange(PAN_DEV), side="right"))(jax.random.split(seeds[5], N_ROW)).reshape((N_ROW, PAN_DEV)).astype(jnp.int32)
    far_pick = draw_far_pick(jax.random.fold_in(seeds[10], 71), 0)
    far_target = plant(jax.random.randint(seeds[7], (N_ROW, ITEMS), 0, LEAF_DEV), jax.random.fold_in(seeds[7], 1), 0, LEAF_DEV - 1).astype(jnp.int32)
    far_offset = plant(jax.random.randint(seeds[8], (N_ROW, ITEMS), 0, OFFSETS), jax.random.fold_in(seeds[8], 1), 0, OFFSETS - 1).astype(jnp.int32)
    translations = scatter_about(seeds[9], (OFFSETS, 2, COEFS, COEFS), (2 * COEFS * ITEMS // LEAF_DEV) ** -0.5, 0.109375)
    return {"right_side": right_side, "near_tiles": near_tiles, "tile_pairs": tile_pairs, "tile_count": tile_count, "panel_expansions": panel_expansions, "leaf_of_panel": leaf_of_panel, "far_pick": far_pick, "far_target": far_target, "far_offset": far_offset, "translations": translations}


EPSILON = 1e-06
HIGHEST = lax.Precision.HIGHEST

def complex_mix(products):
    return jnp.stack([products[0, 0] - products[1, 1], products[0, 1] + products[1, 0]])

def near_field(vector_low, near_tiles, tile_pairs, tile_count):
    blocks = vector_low.astype(jnp.float32).reshape(2, FIELDS, BLOCKS, TILE)
    span_count = 2 * REACH + 1
    device_count = N_GRP * N_ROW * N_COL

    def visit(totals, device):
        row_index = device // N_COL % N_ROW
        pair_codes = lax.dynamic_slice_in_dim(tile_pairs, device * SLOT_DEV, SLOT_DEV)
        tile_block = lax.dynamic_slice_in_dim(near_tiles, device * SLOT_DEV, SLOT_DEV, 1).astype(jnp.float32)
        target = row_index * BLK_DEV + pair_codes // span_count
        source = (target + pair_codes % span_count - REACH) % BLOCKS
        source_rows = jnp.take(blocks, source, axis=2)
        values = complex_mix(jnp.einsum('xstj,ytij->xysti', source_rows, tile_block, precision=HIGHEST))
        live_mask = (jnp.arange(SLOT_DEV, dtype=jnp.int32) < tile_count[device]).astype(jnp.float32)
        values = values * live_mask[None, None, :, None]
        return (totals.at[:, :, target, :].add(values), None)
    initial = jnp.zeros((2, FIELDS, BLOCKS, TILE), jnp.float32)
    totals, unused = lax.scan(visit, initial, jnp.arange(device_count, dtype=jnp.int32))
    return totals.reshape(2, FIELDS, PANELS)

def far_field(vector_low, panel_expansions, leaf_of_panel, far_pick, far_target, far_offset, translations):
    leaf_ids = jnp.arange(LEAF_DEV, dtype=jnp.int32)
    vector_rows = vector_low.reshape(2, FIELDS, N_ROW, PAN_DEV).transpose(2, 0, 1, 3)
    expansion_rows = panel_expansions.reshape(2, N_ROW, PAN_DEV, COEFS).transpose(1, 0, 2, 3)
    translate_wide = translations.astype(jnp.float32)

    def outgoing(operands):
        vector_part, expansion_part, leaf_part = operands
        member = (leaf_part[None, :] == leaf_ids[:, None]).astype(jnp.float32)
        weighted = member[None, None] * vector_part.astype(jnp.float32)[:, :, None, :]
        multipoles = complex_mix(jnp.einsum('xslp,ypk->xyslk', weighted, expansion_part.astype(jnp.float32), precision=HIGHEST))
        return lax.optimization_barrier(multipoles.astype(jnp.bfloat16))
    multipoles = lax.map(outgoing, (vector_rows, expansion_rows, leaf_of_panel))
    flat_leaves = multipoles.transpose(0, 3, 1, 2, 4).reshape(N_ROW * LEAF_DEV, 2, FIELDS, COEFS)
    row_ids = jnp.arange(N_ROW, dtype=jnp.int32)
    slot_ids = jnp.arange(OFFSETS * LEAF_DEV, dtype=jnp.int32)

    def incoming(operands):
        pick_codes, targets, offsets, expansion_part, leaf_part = operands
        chosen = (row_ids[:, None] * LEAF_DEV + pick_codes).reshape(-1)
        item_rows = jnp.take(flat_leaves, chosen, axis=0).astype(jnp.float32)
        selector = (slot_ids[:, None] == (offsets * LEAF_DEV + targets)[None, :]).astype(jnp.float32)
        gathered = jnp.einsum('ai,ixsk->xsak', selector, item_rows, precision=HIGHEST)
        gathered = lax.optimization_barrier(gathered.astype(jnp.bfloat16)).astype(jnp.float32)
        gathered = gathered.reshape(2, FIELDS, OFFSETS, LEAF_DEV, COEFS)
        local_field = complex_mix(jnp.einsum('xsolk,oykj->xyslj', gathered, translate_wide, precision=HIGHEST))
        local_field = lax.optimization_barrier(local_field.astype(jnp.bfloat16)).astype(jnp.float32)
        member = (leaf_part[:, None] == leaf_ids[None, :]).astype(jnp.float32)
        spread = jnp.einsum('pl,xslk->xspk', member, local_field, precision=HIGHEST)
        return complex_mix(jnp.einsum('xspk,ypk->xysp', spread, expansion_part.astype(jnp.float32), precision=HIGHEST))
    result = lax.map(incoming, (far_pick, far_target, far_offset, expansion_rows, leaf_of_panel))
    return result.transpose(1, 2, 0, 3).reshape(2, FIELDS, PANELS)

def inner_product(left, right):
    real_part = lax.optimization_barrier(jnp.sum(left[0] * right[0] + left[1] * right[1], axis=-1))
    imag_part = lax.optimization_barrier(jnp.sum(left[0] * right[1] - left[1] * right[0], axis=-1))
    return jnp.stack([real_part, imag_part])

def scaled_vector(coeff, vector):
    real_coeff = coeff[0][:, None]
    imag_coeff = coeff[1][:, None]
    return jnp.stack([real_coeff * vector[0] - imag_coeff * vector[1], real_coeff * vector[1] + imag_coeff * vector[0]])

def complex_times(left, right):
    return jnp.stack([left[0] * right[0] - left[1] * right[1], left[0] * right[1] + left[1] * right[0]])

def conjugate(value):
    return jnp.stack([value[0], -value[1]])

def small_solve(beta_norm, h_first, h_sub, h_upper, h_middle, h_last):
    radius = jnp.sqrt(h_first[0] * h_first[0] + h_first[1] * h_first[1] + h_sub * h_sub)
    cosine = h_first / radius
    sine_one = h_sub / radius
    upper_row = complex_times(conjugate(cosine), h_upper) + sine_one * h_middle
    lower_row = complex_times(cosine, h_middle) - sine_one * h_upper
    radius_two = jnp.sqrt(lower_row[0] * lower_row[0] + lower_row[1] * lower_row[1] + h_last * h_last)
    cosine_two = lower_row / radius_two
    goal_top = conjugate(cosine) * beta_norm
    goal_mid = -sine_one * beta_norm
    weight_two = conjugate(cosine_two) * (goal_mid / radius_two)
    weight_one = (goal_top - complex_times(upper_row, weight_two)) / radius
    return (weight_one, weight_two)

def reference(right_side, near_tiles, tile_pairs, tile_count, panel_expansions, leaf_of_panel, far_pick, far_target, far_offset, translations):

    def apply_operator(vector):
        vector_low = lax.optimization_barrier(vector.astype(jnp.bfloat16))
        near_image = near_field(vector_low, near_tiles, tile_pairs, tile_count)
        far_image = far_field(vector_low, panel_expansions, leaf_of_panel, far_pick, far_target, far_offset, translations)
        return 0.5 * vector + near_image + far_image
    beta_norm = jnp.sqrt(lax.optimization_barrier(jnp.sum(right_side * right_side, axis=(0, 2))) + EPSILON)
    first_basis = right_side / beta_norm[None, :, None]
    image_one = apply_operator(first_basis)
    h_first = inner_product(first_basis, image_one)
    residue = image_one - scaled_vector(h_first, first_basis)
    h_sub = jnp.sqrt(lax.optimization_barrier(jnp.sum(residue * residue, axis=(0, 2))) + EPSILON)
    second_basis = residue / h_sub[None, :, None]
    image_two = apply_operator(second_basis)
    h_upper = inner_product(first_basis, image_two)
    h_middle = inner_product(second_basis, image_two)
    remainder = image_two - scaled_vector(h_upper, first_basis) - scaled_vector(h_middle, second_basis)
    h_last = jnp.sqrt(lax.optimization_barrier(jnp.sum(remainder * remainder, axis=(0, 2))) + EPSILON)
    weight_one, weight_two = small_solve(beta_norm, h_first, h_sub, h_upper, h_middle, h_last)
    return scaled_vector(weight_one, first_basis) + scaled_vector(weight_two, second_basis)
```

```python
import functools

import jax
import jax.numpy as jnp
from jax import lax
from jax.experimental import pallas as pl
from jax.experimental.pallas import tpu as pltpu
from jax.sharding import PartitionSpec as P

REACH = 2
SPAN = 2 * REACH + 1
OFFSETS = 4
LEAVES = 24
SEND = 2
TILE = 256
LANES = 128
EPSILON = 1e-06
MESH = pl.DeviceIdType.MESH
F32 = jnp.float32
BF16 = jnp.bfloat16


def dot(a, b):
    return jnp.dot(a, b, preferred_element_type=F32)


def dot_nt(a, b):
    return lax.dot_general(a, b, (((1,), (1,)), ((), ())), preferred_element_type=F32)


def iota(shape, dim):
    return lax.broadcasted_iota(jnp.int32, shape, dim)


def one_hot(condition):
    return jnp.where(condition, 1.0, 0.0).astype(BF16)


def c_mul(a, b):
    return (a[0] * b[0] - a[1] * b[1], a[0] * b[1] + a[1] * b[0])


def c_add(a, b):
    return (a[0] + b[0], a[1] + b[1])


def c_scale(a, s):
    return (a[0] * s, a[1] * s)


def c_conj(a):
    return (a[0], -a[1])


def c_square(a):
    return a[0] * a[0] + a[1] * a[1]


def solve(bb, bf, bg, ff, fg, gg):
    beta = jnp.sqrt(bb + EPSILON)
    inv = 1.0 / beta
    inv2 = inv * inv
    bb, ff, gg = bb * inv2, ff * inv2, gg * inv2
    bf, bg, fg = c_scale(bf, inv2), c_scale(bg, inv2), c_scale(fg, inv2)
    h11 = (0.5 * bb + bf[0], bf[1])
    a = (0.5 - h11[0], -h11[1])
    u_square = ff + 2.0 * c_mul(c_conj(a), bf)[0] + c_square(a) * bb
    h21 = jnp.sqrt(jnp.maximum(u_square, 0.0) + EPSILON)
    inv21 = 1.0 / h21
    p = (a[0] + 0.5, a[1])
    q = c_scale(a, 0.5)
    x_b = c_add(c_add(bg, c_mul(p, bf)), c_scale(q, bb))
    x_f = c_add(c_add(fg, c_scale(p, ff)), c_mul(q, c_conj(bf)))
    h12 = c_scale(x_b, inv21)
    h22 = c_scale(c_add(x_f, c_mul(c_conj(a), x_b)), inv21 * inv21)
    p2 = (p[0] - h22[0], p[1] - h22[1])
    ha = c_mul(h22, a)
    q2 = (q[0] - x_b[0] - ha[0], q[1] - x_b[1] - ha[1])
    r_square = (
        gg
        + c_square(p2) * ff
        + c_square(q2) * bb
        + 2.0 * c_mul(p2, c_conj(fg))[0]
        + 2.0 * c_mul(q2, c_conj(bg))[0]
        + 2.0 * c_mul(c_mul(c_conj(p2), q2), c_conj(bf))[0]
    ) * (inv21 * inv21)
    h32 = jnp.sqrt(jnp.maximum(r_square, 0.0) + EPSILON)
    rho1 = jnp.sqrt(c_square(h11) + h21 * h21)
    c1 = c_scale(h11, 1.0 / rho1)
    s1 = h21 / rho1
    r12 = c_add(c_mul(c_conj(c1), h12), c_scale(h22, s1))
    t = c_add(c_mul(c1, h22), c_scale(h12, -s1))
    rho2 = jnp.sqrt(c_square(t) + h32 * h32)
    c2 = c_scale(t, 1.0 / rho2)
    y2 = c_scale(c_conj(c2), -s1 * beta / rho2)
    y1 = c_add(c_scale(c_conj(c1), beta), c_scale(c_mul(r12, y2), -1.0))
    y1 = c_scale(y1, 1.0 / rho1)
    y2 = c_scale(y2, inv21)
    alpha = c_scale(c_add(y1, c_mul(y2, a)), inv)
    return alpha, c_scale(y2, inv)


def kernel(
    sizes,
    pairs,
    count,
    pick,
    leaf,
    target,
    offset,
    rhs_hbm,
    tiles_hbm,
    exps_hbm,
    trans_hbm,
    tail_hbm,
    spread,
    coef,
    rhs,
    tiles,
    exps,
    trans,
    pick_rows,
    pick_sel,
    item_sel,
    weave,
    place,
    source_sel,
    field_sel,
    vec,
    far,
    weighted,
    multi_wide,
    multi,
    multi_out,
    multi_in,
    gathered,
    local,
    woven,
    ext_one,
    src,
    values,
    near_out,
    near_in,
    near_part,
    near_cross,
    halo_out,
    halo_in,
    vec_cross,
    ext_wide,
    ext_out,
    ext_in,
    gram_out,
    gram_in,
    coef_out,
    coef_in,
    load_sem,
    send_sem,
    recv_sem,
    many_send,
    many_recv,
):
    n_grp, n_row, n_col, fields, blocks, slots, coefs = sizes
    grp, row, col = lax.axis_index("grp"), lax.axis_index("row"), lax.axis_index("col")
    other = 1 - grp
    mine = grp * n_col + col
    mates = n_grp * n_col
    up, down = lax.rem(row + 1, n_row), lax.rem(row + n_row - 1, n_row)
    full = blocks + 2 * REACH
    rows = 2 * blocks
    pairs_wide = 2 * coefs
    wide = multi_wide.shape[1]
    strips = wide // LANES
    scope = jax.named_scope

    pltpu.make_async_copy(rhs_hbm, rhs, load_sem.at[0]).start()
    for i in range(rows):
        pltpu.make_async_copy(
            exps_hbm.at[:, :, pl.ds(i * LANES, LANES)], exps.at[i], load_sem.at[1]
        ).start()
    pltpu.make_async_copy(tiles_hbm, tiles, load_sem.at[2]).start()
    parts = trans.shape[0]
    for i in range(parts):
        piece = tail_hbm if i == parts - 1 else trans_hbm.at[:, :, :, pl.ds(i * LANES, LANES)]
        pltpu.make_async_copy(piece, trans.at[i], load_sem.at[3]).start()

    def loaded(ref, sem):
        pltpu.make_async_copy(ref, ref, load_sem.at[sem]).wait()

    barrier = pltpu.get_barrier_semaphore()

    def greet(to):
        pl.semaphore_signal(barrier, inc=1, device_id=to, device_id_type=MESH)

    def greet_row(k, carry):
        greet((grp, lax.rem(row + k, n_row), col))
        return carry

    def greet_mate(k, carry):
        mate = lax.rem(mine + k, mates)
        greet((mate // n_col, row, lax.rem(mate, n_col)))
        return carry

    with scope("greet"):
        lax.fori_loop(1, n_row, greet_row, 0)
        lax.fori_loop(1, mates, greet_mate, 0)
        greet((other, up, col))
        greet((other, down, col))

    def send(source, target, sem, to):
        copy = pltpu.make_async_remote_copy(
            src_ref=source,
            dst_ref=target,
            send_sem=send_sem.at[sem],
            recv_sem=recv_sem.at[sem],
            device_id=to,
            device_id_type=MESH,
        )
        copy.start()
        return copy

    def send_many(source, target, sem, to):
        pltpu.make_async_remote_copy(
            src_ref=source,
            dst_ref=target,
            send_sem=many_send.at[sem],
            recv_sem=many_recv.at[sem],
            device_id=to,
            device_id_type=MESH,
        ).start()

    def await_many(ref, sem):
        pltpu.make_async_copy(ref, ref, many_recv.at[sem]).wait()

    def await_sent(ref, sem):
        pltpu.make_async_copy(ref, ref, many_send.at[sem]).wait()

    with scope("right_side"):
        loaded(rhs, 0)
        for x in range(2):
            for b in range(blocks):
                vec[0, x * blocks + b : x * blocks + b + 1, :] = rhs[
                    x, pl.ds(mine, 1), b * TILE : (b + 1) * TILE
                ]
        for b in range(blocks):
            for x in range(2):
                ext_one[b, x * fields : (x + 1) * fields, :] = rhs[
                    x, :, b * TILE : (b + 1) * TILE
                ].astype(BF16)

    def member(b):
        return iota((LEAVES, TILE), 0) == leaf[:, b * TILE : (b + 1) * TILE]

    def weigh(step):
        for b in range(blocks):
            inside = member(b)
            for x in range(2):
                line = vec[step, x * blocks + b : x * blocks + b + 1, :]
                weighted[x * LEAVES : (x + 1) * LEAVES, b * TILE : (b + 1) * TILE] = jnp.where(
                    inside, line, 0.0
                ).astype(BF16)

    with scope("pick_table"):
        multi_wide[...] = jnp.zeros_like(multi_wide)
        multi[...] = jnp.zeros_like(multi)
        halo_out[...] = jnp.zeros_like(halo_out)
        here_lane = iota(pick.shape, 2) == row
        chosen = jnp.sum(jnp.where(here_lane, pick[...].astype(F32), 0.0), axis=2, keepdims=True)
        pick_rows[...] = jnp.broadcast_to(chosen, pick_rows.shape)
        rows16, lanes16 = iota((16, LANES), 0), iota((16, LANES), 1)
        even16 = lax.rem(rows16, 2) == 0
        base16 = jnp.where(rows16 < 2 * strips, (rows16 // 2) * LEAVES, 2 * TILE)

        def build_pick(d, carry):
            own = pick_rows[d].astype(jnp.int32)
            hit = base16 + jnp.where(even16, own[0:1], own[1:2])
            at = pl.ds(pl.multiple_of(d * 16, 16), 16)
            pick_sel[at, 0:LANES] = one_hot(lanes16 == hit)
            pick_sel[at, LANES:] = one_hot(lanes16 + LANES == hit)
            return carry

        lax.fori_loop(0, n_row, build_pick, 0)
    with scope("weigh"):
        weigh(0)
    panels_of = exps.reshape(rows, pairs_wide, LANES)

    def panel_block(b):
        return jnp.concatenate([panels_of[2 * b], panels_of[2 * b + 1]], axis=1)

    def swapped(value):
        left = pltpu.roll(value, wide - 1, 1)
        right = pltpu.roll(value, 1, 1)
        return left, right

    lane_even = lax.rem(iota((LEAVES, wide), 1), 2) == 0

    def far_send(step):
        with scope("multi"):
            every = jnp.concatenate([panel_block(b) for b in range(blocks)], axis=1)
            multi_wide[:, 0:pairs_wide] = dot_nt(weighted[...], every)
            left, right = swapped(multi_wide[LEAVES:, :])
            total = multi_wide[0:LEAVES, :] + jnp.where(lane_even, -left, right)
            for i in range(strips):
                multi[i * LEAVES : (i + 1) * LEAVES, :] = total[:, i * LANES : (i + 1) * LANES]
            multi_out[step] = dot(pick_sel[...], multi[...].astype(BF16)).astype(BF16)
            here = pl.ds(pl.multiple_of(row * 16, 16), 16)
            multi_in[step, here, :] = multi_out[step, here, :]

        def post(k, carry):
            to = lax.rem(row + k, n_row)
            send_many(
                multi_out.at[step, pl.ds(pl.multiple_of(to * 16, 16), 16)],
                multi_in.at[step, here],
                step,
                (grp, to, col),
            )
            return carry

        with scope("multi_send"):
            lax.fori_loop(1, n_row, post, 0)

    def split(value):
        high = value.astype(BF16)
        return high, (value - high.astype(F32)).astype(BF16)

    def far_local(step):
        with scope("multi_wait"):
            await_many(multi_in.at[step, pl.ds(0, (n_row - 1) * 16)], step)
        if step == 0:
            loaded(trans, 3)
        with scope("translate"):
            picked = dot(item_sel[...], multi_in[step])
            pieces = trans.reshape(parts, OFFSETS, pairs_wide, LANES)
            total = None
            for o in range(OFFSETS):
                lines = jnp.concatenate(
                    [
                        picked[(i * OFFSETS + o) * LEAVES : (i * OFFSETS + o + 1) * LEAVES]
                        for i in range(strips)
                    ],
                    axis=1,
                )
                left, right = swapped(lines)
                for x, value in enumerate(
                    (jnp.where(lane_even, lines, -lines), jnp.where(lane_even, left, right))
                ):
                    local[x * LEAVES : (x + 1) * LEAVES, :] = value
                high, low = split(local[...])
                gathered[0 : 2 * LEAVES, :] = high
                gathered[2 * LEAVES :, :] = low
                matrix = jnp.concatenate([pieces[i, o] for i in range(parts)], axis=1)
                term = dot(gathered[:, 0:pairs_wide], matrix)
                total = term if total is None else total + term
            field = total[0 : 2 * LEAVES] + total[2 * LEAVES :]
            real, imag = field[0:LEAVES], field[LEAVES:]
            stacked = []
            for i in range(parts):
                r, m = (v[:, i * LANES : (i + 1) * LANES] for v in (real, imag))
                lines = jnp.concatenate(
                    [jnp.concatenate([r, -m], axis=1), jnp.concatenate([m, r], axis=1)], axis=0
                )
                stacked.extend(split(lines))
            mixed = dot(jnp.concatenate(stacked, axis=0), weave[...]).astype(BF16)
            for i in range(parts):
                woven[:, i * TILE : (i + 1) * TILE] = mixed[
                    i * 4 * LEAVES : (i + 1) * 4 * LEAVES
                ]

    def far_image():
        with scope("evaluate"):
            lines = woven[:, 0:pairs_wide]
            for b in range(blocks):
                found = dot(lines, panel_block(b))
                found = found[0 : 2 * LEAVES] + found[2 * LEAVES :]
                inside = member(b)
                for x in range(2):
                    value = jnp.where(inside, found[x * LEAVES : (x + 1) * LEAVES], 0.0)
                    at = x * blocks + b
                    far[at : at + 1, :] = jnp.sum(value, axis=0, keepdims=True)

    with scope("near_table"):
        targets = [pairs[t] // SPAN for t in range(slots)]
        sources = []
        for t in range(slots):
            rel = targets[t] + lax.rem(pairs[t], SPAN) - REACH
            inner = jnp.where(rel >= blocks, rel + REACH, rel)
            sources.append(jnp.where(rel < 0, rel + blocks + REACH, inner))
        half = 2 * slots * fields
        k_iota = iota((1, 2 * half), 1)
        k_slot = lax.rem(k_iota, slots * fields) // fields
        k_field = lax.rem(k_iota, fields)
        k_part = lax.rem(k_iota, half) // (slots * fields)
        k_target = jnp.full_like(k_iota, -1)
        for t in range(slots):
            goal = jnp.where(t < count[0], targets[t], -1)
            k_target = jnp.where(k_slot == t, goal, k_target)
        width = n_grp * rows
        k_row = lax.rem(k_field, n_col) * width + (k_field // n_col) * rows + k_part * blocks
        k_row = jnp.where(k_target < 0, -1, k_row + k_target)
        place[...] = one_hot(iota(place.shape, 0) == k_row)
        e_iota = iota((2 * fields, source_sel.shape[1]), 1)
        e_rows = iota(e_iota.shape, 0)
        e_group = lax.rem(e_iota // (2 * full) + grp, 2)
        e_field = e_group * n_col + e_iota // (4 * full)
        e_own = e_field + lax.rem(e_iota // full, 2) * fields == e_rows
        e_block = lax.rem(e_iota, full)
        for t in range(slots):
            source_sel[t * 2 * fields : (t + 1) * 2 * fields, :] = one_hot(
                e_own & (e_block == sources[t])
            )
        for b in range(blocks):
            field_sel[b * 2 * fields : (b + 1) * 2 * fields, :] = one_hot(e_own & (e_block == b))

    def near_send(step):
        with scope("near"):
            for t in range(slots):
                by_real = dot_nt(src[t], tiles[0, t])
                by_imag = dot_nt(src[t], tiles[1, t])
                real = by_real[0:fields] - by_imag[fields:]
                imag = by_imag[0:fields] + by_real[fields:]
                for x, value in enumerate((real, imag)):
                    start = (x * slots + t) * fields
                    high, low = split(value)
                    values[start : start + fields, :] = high
                    values[half + start : half + start + fields, :] = low
            image = dot(place[...], values[...]).astype(BF16)
            for c in range(n_col):
                near_out[step, c] = image[c * width : (c + 1) * width]
            near_in[step, col] = near_out[step, col]

        def post(k, carry):
            to = lax.rem(col + k, n_col)
            send_many(near_out.at[step, to], near_in.at[step, col], 2 + step, (grp, row, to))
            return carry

        with scope("near_send"):
            lax.fori_loop(1, n_col, post, 0)

    def near_sum(step):
        with scope("near_wait"):
            await_many(near_in.at[step, pl.ds(0, n_col - 1)], 2 + step)
        with scope("near_sum"):
            near_part[step] = jnp.sum(near_in[step].astype(F32), axis=0)
            start = pl.multiple_of(other * rows, 8)
            return send(
                near_part.at[step, pl.ds(start, rows)],
                near_cross.at[step],
                2 + step,
                (other, row, col),
            )

    def image(step, cross):
        with scope("cross_wait"):
            cross.wait_recv()
        start = pl.multiple_of(grp * rows, 8)
        vec[step + 1] = near_part[step, pl.ds(start, rows), :] + near_cross[step] + far[...]

    with scope("barrier_wait"):
        pl.semaphore_wait(barrier, (n_row - 1) + (mates - 1) + 2)
    halo_one = [
        send(ext_one.at[pl.ds(blocks - 2, 2)], ext_one.at[pl.ds(blocks, 2)], 0, (grp, up, col)),
        send(ext_one.at[pl.ds(0, 2)], ext_one.at[pl.ds(blocks + 2, 2)], 1, (grp, down, col)),
    ]

    with scope("exps_wait"):
        loaded(exps, 1)
    far_send(0)
    with scope("halo_wait"):
        loaded(tiles, 2)
        for copy in halo_one:
            copy.wait_recv()
    for t in range(slots):
        src[t] = ext_one[sources[t]]
    near_send(0)
    with scope("item_table"):
        weave[...] = one_hot(
            iota(weave.shape, 1)
            == 2 * lax.rem(iota(weave.shape, 0), LANES) + iota(weave.shape, 0) // LANES
        )
        keys = (offset[...] * LEAVES + target[...]).astype(F32).astype(BF16)
        item = iota((keys.shape[1], 16 * n_row), 0)
        place_at = iota((keys.shape[1], 16 * n_row), 1)
        repeat = one_hot(
            (item // SEND == place_at // 16) & (lax.rem(item, SEND) == lax.rem(place_at, SEND))
        )
        spread_keys = dot(jnp.broadcast_to(keys, (8, keys.shape[1])), repeat)[0:1]
        strip = lax.rem(iota(spread_keys.shape, 1), 16) // SEND
        hits = spread_keys.astype(jnp.int32) + strip * (OFFSETS * LEAVES)
        item_iota = iota((16, 16 * n_row), 0)
        src_rows = item_sel.shape[0]
        for i in range(src_rows // 16):
            item_sel[i * 16 : (i + 1) * 16, :] = one_hot(item_iota + i * 16 == hits)
    far_local(0)
    cross_one = near_sum(0)
    far_image()
    image(0, cross_one)

    with scope("halo_send"):
        vec_send = send(vec.at[1], vec_cross, 4, (other, row, col))
        for x in range(2):
            last = vec[1, x * blocks + blocks - 2 : (x + 1) * blocks, :]
            halo_out[0, x * 2 : x * 2 + 2, :] = last
            halo_out[1, x * 2 : x * 2 + 2, :] = vec[1, x * blocks : x * blocks + 2, :]
        halo_two = [
            send(halo_out.at[0], halo_in.at[0, 0], 5, (grp, up, col)),
            send(halo_out.at[1], halo_in.at[0, 1], 6, (grp, down, col)),
            send(halo_out.at[0], halo_in.at[1, 0], 7, (other, up, col)),
            send(halo_out.at[1], halo_in.at[1, 1], 8, (other, down, col)),
        ]
        weigh(1)
    far_send(1)
    with scope("vec_wait"):
        vec_send.wait_recv()
        for copy in halo_two:
            copy.wait_recv()
    with scope("extend"):
        for f in range(2):
            for x in range(2):
                lines = (vec[1] if f == 0 else vec_cross[...])[x * blocks : (x + 1) * blocks]
                ext_wide[f, x * full : x * full + blocks, :] = lines
                for side in range(2):
                    start = x * full + blocks + 2 * side
                    ext_wide[f, start : start + 2, :] = halo_in[f, side, x * 2 : x * 2 + 2, :]
        for f in range(2):
            ext_out[0, f], ext_out[1, f] = split(ext_wide[f])
        for i in range(2):
            ext_in[i, col] = ext_out[i]

    def post_ext(i):
        def post(k, carry):
            to = lax.rem(col + k, n_col)
            send_many(ext_out.at[i], ext_in.at[i, col], 4 + i, (grp, row, to))
            return carry

        lax.fori_loop(1, n_col, post, 0)

    def blocks_in(i):
        return jnp.concatenate([ext_in[i, c, f] for c in range(n_col) for f in range(2)], axis=0)

    post_ext(0)
    with scope("ext_wait"):
        await_many(ext_in.at[0, pl.ds(0, n_col - 1)], 4)
    with scope("source"):
        chosen_blocks = dot(source_sel[...], blocks_in(0)).astype(BF16)
        for t in range(slots):
            src[t] = chosen_blocks[t * 2 * fields : (t + 1) * 2 * fields]
    near_send(1)
    post_ext(1)
    far_local(1)
    cross_two = near_sum(1)
    far_image()
    image(1, cross_two)

    with scope("gram"):
        lane = iota((1, LANES), 1)
        v = [vec[i] for i in range(3)]
        turned = [
            jnp.concatenate([vec[i, blocks:, :], -vec[i, 0:blocks, :]], axis=0) for i in range(3)
        ]
        products = [
            v[0] * v[0],
            v[0] * v[1],
            v[0] * turned[1],
            v[0] * v[2],
            v[0] * turned[2],
            v[1] * v[1],
            v[1] * v[2],
            v[1] * turned[2],
            v[2] * v[2],
        ]
        packed = jnp.zeros((1, LANES), F32)
        for i, product in enumerate(products):
            total = jnp.sum(jnp.sum(product, axis=0, keepdims=True), axis=1, keepdims=True)
            packed = jnp.where(lane == i, total, packed)
        gram_out[...] = packed
        gram_in[row] = packed

    def post_gram(k, carry):
        send_many(gram_out, gram_in.at[row], 6, (grp, lax.rem(row + k, n_row), col))
        return carry

    with scope("gram_send"):
        lax.fori_loop(1, n_row, post_gram, 0)
    with scope("spread"):
        await_many(ext_in.at[1, pl.ds(0, n_col - 1)], 5)
        all_fields = dot(field_sel[...], blocks_in(0)) + dot(field_sel[...], blocks_in(1))
        for b in range(blocks):
            for x in range(2):
                start = (b * 2 + x) * fields
                spread[x, :, b * TILE : (b + 1) * TILE] = all_fields[start : start + fields]
    with scope("gram_wait"):
        await_many(gram_in.at[pl.ds(0, n_row - 1)], 6)
    with scope("solve"):
        total = jnp.sum(gram_in[...], axis=0)
        g = [jnp.sum(jnp.where(lane == i, total, 0.0), axis=1, keepdims=True) for i in range(9)]
        alpha, gamma = solve(g[0], (g[1], g[2]), (g[3], g[4]), g[5], (g[6], g[7]), g[8])
        packed = jnp.zeros((1, LANES), F32)
        for i, value in enumerate((*alpha, *gamma)):
            packed = jnp.where(lane == i, value, packed)
        coef_out[...] = packed
        coef_in[mine] = packed

    def post_coef(k, carry):
        mate = lax.rem(mine + k, mates)
        to = (mate // n_col, row, lax.rem(mate, n_col))
        send_many(coef_out, coef_in.at[mine], 7, to)
        return carry

    lax.fori_loop(1, mates, post_coef, 0)
    with scope("coef_wait"):
        await_many(coef_in.at[pl.ds(0, mates - 1)], 7)
    for s in range(fields):
        coef[s : s + 1, :] = coef_in[s]

    with scope("sent_wait"):
        for copy in (*halo_one, cross_one, vec_send, *halo_two, cross_two):
            copy.wait_send()
        for step in range(2):
            await_sent(multi_in.at[step, pl.ds(0, (n_row - 1) * 16)], step)
            await_sent(near_in.at[step, pl.ds(0, n_col - 1)], 2 + step)
            await_sent(ext_in.at[step, pl.ds(0, n_col - 1)], 4 + step)
        await_sent(gram_in.at[pl.ds(0, n_row - 1)], 6)
        await_sent(coef_in.at[pl.ds(0, mates - 1)], 7)


def local_part(
    right_side,
    near_tiles,
    tile_pairs,
    tile_count,
    panel_expansions,
    leaf_of_panel,
    far_pick,
    far_target,
    far_offset,
    translations,
):
    n_grp, n_row, n_col = (lax.axis_size(axis) for axis in ("grp", "row", "col"))
    fields, panels = right_side.shape[1:]
    blocks = panels // TILE
    slots = near_tiles.shape[1]
    coefs = panel_expansions.shape[2]
    parts = pl.cdiv(coefs, LANES)
    strips = pl.cdiv(2 * coefs, LANES)
    exps = jnp.transpose(panel_expansions, (2, 0, 1))
    trans = jnp.transpose(translations, (0, 2, 1, 3))
    whole_part = (parts - 1) * LANES
    spare = [(0, 0)] * 3 + [(0, parts * LANES - coefs)]
    tail = jnp.pad(trans[..., whole_part:], spare)
    full = blocks + 2 * REACH
    rows = 2 * blocks
    depth = n_col * 4 * full
    vm = pltpu.VMEM
    scratch = [
        vm(right_side.shape, F32),
        vm(near_tiles.shape, BF16),
        vm((panels // LANES, coefs, 2, LANES), BF16),
        vm((parts, OFFSETS, coefs, 2, LANES), BF16),
        vm((n_row, SEND, LANES), F32),
        vm((16 * n_row, TILE), BF16),
        vm((strips * OFFSETS * LEAVES, 16 * n_row), BF16),
        vm((TILE, TILE), BF16),
        vm((n_col * n_grp * rows, 4 * slots * fields), BF16),
        vm((slots * 2 * fields, depth), BF16),
        vm((blocks * 2 * fields, depth), BF16),
        vm((3, rows, TILE), F32),
        vm((rows, TILE), F32),
        vm((2 * LEAVES, panels), BF16),
        vm((2 * LEAVES, strips * LANES), F32),
        vm((TILE, LANES), F32),
        vm((2, 16 * n_row, LANES), BF16),
        vm((2, 16 * n_row, LANES), BF16),
        vm((4 * LEAVES, strips * LANES), BF16),
        vm((2 * LEAVES, strips * LANES), F32),
        vm((4 * LEAVES, parts * TILE), BF16),
        vm((full, 2 * fields, TILE), BF16),
        vm((slots, 2 * fields, TILE), BF16),
        vm((4 * slots * fields, TILE), BF16),
        vm((2, n_col, n_grp * rows, TILE), BF16),
        vm((2, n_col, n_grp * rows, TILE), BF16),
        vm((2, n_grp * rows, TILE), F32),
        vm((2, rows, TILE), F32),
        vm((2, 8, TILE), F32),
        vm((2, 2, 8, TILE), F32),
        vm((rows, TILE), F32),
        vm((2, 2 * full, TILE), F32),
        vm((2, 2, 2 * full, TILE), BF16),
        vm((2, n_col, 2, 2 * full, TILE), BF16),
        vm((1, LANES), F32),
        vm((n_row, 1, LANES), F32),
        vm((1, LANES), F32),
        vm((n_grp * n_col, 1, LANES), F32),
        pltpu.SemaphoreType.DMA((4,)),
        pltpu.SemaphoreType.DMA((9,)),
        pltpu.SemaphoreType.DMA((9,)),
        pltpu.SemaphoreType.DMA((8,)),
        pltpu.SemaphoreType.DMA((8,)),
    ]
    smem = pl.BlockSpec(memory_space=pltpu.SMEM)
    whole = pl.BlockSpec(memory_space=pltpu.VMEM)
    hbm = pl.BlockSpec(memory_space=pl.ANY)
    sizes = (n_grp, n_row, n_col, fields, blocks, slots, coefs)
    spread, coef = pl.pallas_call(
        functools.partial(kernel, sizes),
        out_shape=[
            jax.ShapeDtypeStruct(right_side.shape, F32),
            jax.ShapeDtypeStruct((fields, LANES), F32),
        ],
        in_specs=[smem, smem, whole, whole, whole, whole, hbm, hbm, hbm, hbm, hbm],
        out_specs=[whole, whole],
        scratch_shapes=scratch,
        compiler_params=pltpu.CompilerParams(
            collective_id=0, has_side_effects=True, vmem_limit_bytes=60 << 20
        ),
    )(
        tile_pairs,
        tile_count,
        jnp.transpose(far_pick, (0, 2, 1)),
        leaf_of_panel,
        far_target,
        far_offset,
        right_side,
        near_tiles,
        exps,
        trans,
        tail,
    )
    c = [coef[:, i : i + 1] for i in range(4)]
    real = c[0] * right_side[0] - c[1] * right_side[1] + c[2] * spread[0] - c[3] * spread[1]
    imag = c[0] * right_side[1] + c[1] * right_side[0] + c[2] * spread[1] + c[3] * spread[0]
    return jnp.stack([real, imag])


def solution(mesh):
    return jax.shard_map(
        local_part,
        mesh=mesh,
        in_specs=(
            P(None, None, "row"),
            P(None, ("grp", "row", "col"), None, None),
            P(("grp", "row", "col")),
            P(("grp", "row", "col")),
            P(None, "row", None),
            P("row", None),
            P(),
            P("row", None),
            P("row", None),
            P(),
        ),
        out_specs=P(None, None, "row"),
        check_vma=False,
    )
```

```python
import functools

import jax
import jax.numpy as jnp
from jax import lax
from jax.experimental import pallas as pl
from jax.experimental.pallas import tpu as pltpu
from jax.sharding import PartitionSpec as P

REACH = 2
SPAN = 2 * REACH + 1
OFFSETS = 4
LEAVES = 24
SEND = 2
TILE = 256
LANES = 128
EPSILON = 1e-06
MESH = pl.DeviceIdType.MESH
F32 = jnp.float32
BF16 = jnp.bfloat16


def dot(a, b):
    return jnp.dot(a, b, preferred_element_type=F32)


def dot_nt(a, b):
    return lax.dot_general(a, b, (((1,), (1,)), ((), ())), preferred_element_type=F32)


def iota(shape, dim):
    return lax.broadcasted_iota(jnp.int32, shape, dim)


def one_hot(condition):
    return jnp.where(condition, 1.0, 0.0).astype(BF16)


def c_mul(a, b):
    return (a[0] * b[0] - a[1] * b[1], a[0] * b[1] + a[1] * b[0])


def c_add(a, b):
    return (a[0] + b[0], a[1] + b[1])


def c_scale(a, s):
    return (a[0] * s, a[1] * s)


def c_conj(a):
    return (a[0], -a[1])


def c_square(a):
    return a[0] * a[0] + a[1] * a[1]


def solve(bb, bf, bg, ff, fg, gg):
    beta = jnp.sqrt(bb + EPSILON)
    inv = 1.0 / beta
    inv2 = inv * inv
    bb, ff, gg = bb * inv2, ff * inv2, gg * inv2
    bf, bg, fg = c_scale(bf, inv2), c_scale(bg, inv2), c_scale(fg, inv2)
    h11 = (0.5 * bb + bf[0], bf[1])
    a = (0.5 - h11[0], -h11[1])
    u_square = ff + 2.0 * c_mul(c_conj(a), bf)[0] + c_square(a) * bb
    h21 = jnp.sqrt(jnp.maximum(u_square, 0.0) + EPSILON)
    inv21 = 1.0 / h21
    p = (a[0] + 0.5, a[1])
    q = c_scale(a, 0.5)
    x_b = c_add(c_add(bg, c_mul(p, bf)), c_scale(q, bb))
    x_f = c_add(c_add(fg, c_scale(p, ff)), c_mul(q, c_conj(bf)))
    h12 = c_scale(x_b, inv21)
    h22 = c_scale(c_add(x_f, c_mul(c_conj(a), x_b)), inv21 * inv21)
    p2 = (p[0] - h22[0], p[1] - h22[1])
    ha = c_mul(h22, a)
    q2 = (q[0] - x_b[0] - ha[0], q[1] - x_b[1] - ha[1])
    r_square = (
        gg
        + c_square(p2) * ff
        + c_square(q2) * bb
        + 2.0 * c_mul(p2, c_conj(fg))[0]
        + 2.0 * c_mul(q2, c_conj(bg))[0]
        + 2.0 * c_mul(c_mul(c_conj(p2), q2), c_conj(bf))[0]
    ) * (inv21 * inv21)
    h32 = jnp.sqrt(jnp.maximum(r_square, 0.0) + EPSILON)
    rho1 = jnp.sqrt(c_square(h11) + h21 * h21)
    c1 = c_scale(h11, 1.0 / rho1)
    s1 = h21 / rho1
    r12 = c_add(c_mul(c_conj(c1), h12), c_scale(h22, s1))
    t = c_add(c_mul(c1, h22), c_scale(h12, -s1))
    rho2 = jnp.sqrt(c_square(t) + h32 * h32)
    c2 = c_scale(t, 1.0 / rho2)
    y2 = c_scale(c_conj(c2), -s1 * beta / rho2)
    y1 = c_add(c_scale(c_conj(c1), beta), c_scale(c_mul(r12, y2), -1.0))
    y1 = c_scale(y1, 1.0 / rho1)
    y2 = c_scale(y2, inv21)
    alpha = c_scale(c_add(y1, c_mul(y2, a)), inv)
    return alpha, c_scale(y2, inv)


def kernel(
    sizes,
    pairs,
    count,
    pick,
    leaf,
    target,
    offset,
    rhs_hbm,
    tiles_hbm,
    exps_hbm,
    trans_hbm,
    tail_hbm,
    out,
    rhs,
    tiles,
    exps,
    trans,
    pick_rows,
    pick_sel,
    item_sel,
    weave,
    place,
    source_sel,
    field_sel,
    vec,
    far,
    weighted,
    multi_wide,
    multi,
    multi_out,
    multi_in,
    gathered,
    local,
    woven,
    ext_one,
    src,
    values,
    near_out,
    near_in,
    near_part,
    near_cross,
    halo_out,
    halo_in,
    vec_cross,
    ext_wide,
    ext_out,
    ext_in,
    spread,
    coef,
    gram_out,
    gram_in,
    cross_out,
    cross_in,
    coef_out,
    coef_in,
    load_sem,
    send_sem,
    recv_sem,
    many_send,
    many_recv,
):
    n_grp, n_row, n_col, fields, blocks, slots, coefs = sizes
    grp, row, col = lax.axis_index("grp"), lax.axis_index("row"), lax.axis_index("col")
    other = 1 - grp
    mine = grp * n_col + col
    chips, depth_z = n_row // 12, 6
    along = grp * depth_z + lax.rem(row // 2, depth_z)
    beside = (row // (2 * depth_z)) * 2 + lax.rem(row, 2)
    up, down = lax.rem(row + 1, n_row), lax.rem(row + n_row - 1, n_row)
    full = blocks + 2 * REACH
    rows = 2 * blocks
    pairs_wide = 2 * coefs
    wide = multi_wide.shape[1]
    strips = wide // LANES
    scope = jax.named_scope

    pltpu.make_async_copy(rhs_hbm, rhs, load_sem.at[0]).start()
    for i in range(rows):
        pltpu.make_async_copy(
            exps_hbm.at[:, :, pl.ds(i * LANES, LANES)], exps.at[i], load_sem.at[1]
        ).start()
    pltpu.make_async_copy(tiles_hbm, tiles, load_sem.at[2]).start()
    parts = trans.shape[0]
    for i in range(parts):
        piece = tail_hbm if i == parts - 1 else trans_hbm.at[:, :, :, pl.ds(i * LANES, LANES)]
        pltpu.make_async_copy(piece, trans.at[i], load_sem.at[3]).start()

    def loaded(ref, sem):
        pltpu.make_async_copy(ref, ref, load_sem.at[sem]).wait()

    barrier = pltpu.get_barrier_semaphore()

    def greet(to):
        pl.semaphore_signal(barrier, inc=1, device_id=to, device_id_type=MESH)

    def greet_row(k, carry):
        greet((grp, lax.rem(row + k, n_row), col))
        return carry

    def greet_col(k, carry):
        greet((grp, row, lax.rem(col + k, n_col)))
        return carry

    def row_of(side, z):
        return (side // 2) * (2 * depth_z) + z * 2 + lax.rem(side, 2)

    def greet_other(z, carry):
        greet((other, row_of(beside, z), col))
        return carry

    with scope("greet"):
        lax.fori_loop(1, n_row, greet_row, 0)
        lax.fori_loop(0, depth_z, greet_other, 0)
        lax.fori_loop(1, n_col, greet_col, 0)
        greet((other, up, col))
        greet((other, down, col))

    def send(source, target, sem, to):
        copy = pltpu.make_async_remote_copy(
            src_ref=source,
            dst_ref=target,
            send_sem=send_sem.at[sem],
            recv_sem=recv_sem.at[sem],
            device_id=to,
            device_id_type=MESH,
        )
        copy.start()
        return copy

    def send_many(source, target, sem, to):
        pltpu.make_async_remote_copy(
            src_ref=source,
            dst_ref=target,
            send_sem=many_send.at[sem],
            recv_sem=many_recv.at[sem],
            device_id=to,
            device_id_type=MESH,
        ).start()

    def await_many(ref, sem):
        pltpu.make_async_copy(ref, ref, many_recv.at[sem]).wait()

    def await_sent(ref, sem):
        pltpu.make_async_copy(ref, ref, many_send.at[sem]).wait()

    with scope("right_side"):
        loaded(rhs, 0)
        for x in range(2):
            for b in range(blocks):
                vec[0, x * blocks + b : x * blocks + b + 1, :] = rhs[
                    x, pl.ds(mine, 1), b * TILE : (b + 1) * TILE
                ]
        for b in range(blocks):
            for x in range(2):
                ext_one[b, x * fields : (x + 1) * fields, :] = rhs[
                    x, :, b * TILE : (b + 1) * TILE
                ].astype(BF16)

    def member(b):
        return iota((LEAVES, TILE), 0) == leaf[:, b * TILE : (b + 1) * TILE]

    def weigh(step):
        for b in range(blocks):
            inside = member(b)
            for x in range(2):
                line = vec[step, x * blocks + b : x * blocks + b + 1, :]
                weighted[x * LEAVES : (x + 1) * LEAVES, b * TILE : (b + 1) * TILE] = jnp.where(
                    inside, line, 0.0
                ).astype(BF16)

    with scope("pick_table"):
        multi_wide[...] = jnp.zeros_like(multi_wide)
        multi[...] = jnp.zeros_like(multi)
        halo_out[...] = jnp.zeros_like(halo_out)
        here_lane = iota(pick.shape, 2) == row
        chosen = jnp.sum(jnp.where(here_lane, pick[...].astype(F32), 0.0), axis=2, keepdims=True)
        pick_rows[...] = jnp.broadcast_to(chosen, pick_rows.shape)
        rows16, lanes16 = iota((16, LANES), 0), iota((16, LANES), 1)
        even16 = lax.rem(rows16, 2) == 0
        base16 = jnp.where(rows16 < 2 * strips, (rows16 // 2) * LEAVES, 2 * TILE)

        def build_pick(d, carry):
            own = pick_rows[d].astype(jnp.int32)
            hit = base16 + jnp.where(even16, own[0:1], own[1:2])
            at = pl.ds(pl.multiple_of(d * 16, 16), 16)
            pick_sel[at, 0:LANES] = one_hot(lanes16 == hit)
            pick_sel[at, LANES:] = one_hot(lanes16 + LANES == hit)
            return carry

        lax.fori_loop(0, n_row, build_pick, 0)
    with scope("weigh"):
        weigh(0)
    panels_of = exps.reshape(rows, pairs_wide, LANES)

    def panel_block(b):
        return jnp.concatenate([panels_of[2 * b], panels_of[2 * b + 1]], axis=1)

    def swapped(value):
        left = pltpu.roll(value, wide - 1, 1)
        right = pltpu.roll(value, 1, 1)
        return left, right

    lane_even = lax.rem(iota((LEAVES, wide), 1), 2) == 0

    here = pl.ds(pl.multiple_of(row * 16, 16), 16)

    def far_multi(step):
        with scope("multi"):
            total = None
            for b in range(blocks):
                term = dot_nt(weighted[:, b * TILE : (b + 1) * TILE], panel_block(b))
                total = term if total is None else total + term
            multi_wide[:, 0:pairs_wide] = total
            left, right = swapped(multi_wide[LEAVES:, :])
            total = multi_wide[0:LEAVES, :] + jnp.where(lane_even, -left, right)
            for i in range(strips):
                multi[i * LEAVES : (i + 1) * LEAVES, :] = total[:, i * LANES : (i + 1) * LANES]
            multi_out[step] = dot(pick_sel[...], multi[...].astype(BF16)).astype(BF16)
            multi_in[step, here, :] = multi_out[step, here, :]

    def far_post(step):
        def post(k, carry):
            to = lax.rem(row + 1 + lax.rem(k + n_row // 3, n_row - 1), n_row)
            send_many(
                multi_out.at[step, pl.ds(pl.multiple_of(to * 16, 16), 16)],
                multi_in.at[step, here],
                step,
                (grp, to, col),
            )
            return carry

        with scope("multi_send"):
            lax.fori_loop(0, n_row - 1, post, 0)

    def split(value):
        high = value.astype(BF16)
        return high, (value - high.astype(F32)).astype(BF16)

    def far_local(step):
        with scope("multi_wait"):
            await_many(multi_in.at[step, pl.ds(0, (n_row - 1) * 16)], step)
        if step == 0:
            loaded(trans, 3)
        with scope("translate"):
            picked = dot(item_sel[...], multi_in[step])
            pieces = trans.reshape(parts, OFFSETS, pairs_wide, LANES)
            total = None
            for o in range(OFFSETS):
                lines = jnp.concatenate(
                    [
                        picked[(i * OFFSETS + o) * LEAVES : (i * OFFSETS + o + 1) * LEAVES]
                        for i in range(strips)
                    ],
                    axis=1,
                )
                left, right = swapped(lines)
                for x, value in enumerate(
                    (jnp.where(lane_even, lines, -lines), jnp.where(lane_even, left, right))
                ):
                    local[x * LEAVES : (x + 1) * LEAVES, :] = value
                high, low = split(local[...])
                gathered[0 : 2 * LEAVES, :] = high
                gathered[2 * LEAVES :, :] = low
                matrix = jnp.concatenate([pieces[i, o] for i in range(parts)], axis=1)
                term = dot(gathered[:, 0:pairs_wide], matrix)
                total = term if total is None else total + term
            field = total[0 : 2 * LEAVES] + total[2 * LEAVES :]
            real, imag = field[0:LEAVES], field[LEAVES:]
            stacked = []
            for i in range(parts):
                r, m = (v[:, i * LANES : (i + 1) * LANES] for v in (real, imag))
                lines = jnp.concatenate(
                    [jnp.concatenate([r, -m], axis=1), jnp.concatenate([m, r], axis=1)], axis=0
                )
                stacked.extend(split(lines))
            mixed = dot(jnp.concatenate(stacked, axis=0), weave[...]).astype(BF16)
            for i in range(parts):
                woven[:, i * TILE : (i + 1) * TILE] = mixed[
                    i * 4 * LEAVES : (i + 1) * 4 * LEAVES
                ]

    def far_image():
        with scope("evaluate"):
            lines = woven[:, 0:pairs_wide]
            for b in range(blocks):
                found = dot(lines, panel_block(b))
                found = found[0 : 2 * LEAVES] + found[2 * LEAVES :]
                inside = member(b)
                for x in range(2):
                    value = jnp.where(inside, found[x * LEAVES : (x + 1) * LEAVES], 0.0)
                    at = x * blocks + b
                    far[at : at + 1, :] = jnp.sum(value, axis=0, keepdims=True)

    def near_send(step):
        with scope("near"):
            for t in range(slots):
                by_real = dot_nt(src[t], tiles[0, t])
                by_imag = dot_nt(src[t], tiles[1, t])
                real = by_real[0:fields] - by_imag[fields:]
                imag = by_imag[0:fields] + by_real[fields:]
                for x, value in enumerate((real, imag)):
                    start = (x * slots + t) * fields
                    high, low = split(value)
                    values[start : start + fields, :] = high
                    values[half + start : half + start + fields, :] = low
            image = dot(place[...], values[...]).astype(BF16)
            for c in range(n_col):
                near_out[step, c] = image[c * width : (c + 1) * width]
            near_in[step, col] = near_out[step, col]

        def post(k, carry):
            to = lax.rem(col + k, n_col)
            send_many(near_out.at[step, to], near_in.at[step, col], 2 + step, (grp, row, to))
            return carry

        with scope("near_send"):
            lax.fori_loop(1, n_col, post, 0)

    def near_sum(step):
        with scope("near_wait"):
            await_many(near_in.at[step, pl.ds(0, n_col - 1)], 2 + step)
        with scope("near_sum"):
            near_part[step] = jnp.sum(near_in[step].astype(F32), axis=0)
            start = pl.multiple_of(other * rows, 8)
            return send(
                near_part.at[step, pl.ds(start, rows)],
                near_cross.at[step],
                2 + step,
                (other, row, col),
            )

    def image(step, cross):
        with scope("cross_wait"):
            cross.wait_recv()
        start = pl.multiple_of(grp * rows, 8)
        vec[step + 1] = near_part[step, pl.ds(start, rows), :] + near_cross[step] + far[...]

    with scope("exps_wait"):
        loaded(exps, 1)
    far_multi(0)
    with scope("barrier_wait"):
        pl.semaphore_wait(barrier, (n_row - 1) + depth_z + (n_col - 1) + 2)
    halo_one = [
        send(ext_one.at[pl.ds(blocks - 2, 2)], ext_one.at[pl.ds(blocks, 2)], 0, (grp, up, col)),
        send(ext_one.at[pl.ds(0, 2)], ext_one.at[pl.ds(blocks + 2, 2)], 1, (grp, down, col)),
    ]
    far_post(0)

    with scope("near_table"):
        targets = [pairs[t] // SPAN for t in range(slots)]
        sources = []
        for t in range(slots):
            rel = targets[t] + lax.rem(pairs[t], SPAN) - REACH
            inner = jnp.where(rel >= blocks, rel + REACH, rel)
            sources.append(jnp.where(rel < 0, rel + blocks + REACH, inner))
        half = 2 * slots * fields
        k_iota = iota((1, 2 * half), 1)
        k_slot = lax.rem(k_iota, slots * fields) // fields
        k_field = lax.rem(k_iota, fields)
        k_part = lax.rem(k_iota, half) // (slots * fields)
        k_target = jnp.full_like(k_iota, -1)
        for t in range(slots):
            goal = jnp.where(t < count[0], targets[t], -1)
            k_target = jnp.where(k_slot == t, goal, k_target)
        width = n_grp * rows
        k_row = lax.rem(k_field, n_col) * width + (k_field // n_col) * rows + k_part * blocks
        k_row = jnp.where(k_target < 0, -1, k_row + k_target)
        place[...] = one_hot(iota(place.shape, 0) == k_row)
    with scope("halo_wait"):
        loaded(tiles, 2)
        for copy in halo_one:
            copy.wait_recv()
    for t in range(slots):
        src[t] = ext_one[sources[t]]
    near_send(0)
    with scope("item_table"):
        weave[...] = one_hot(
            iota(weave.shape, 1)
            == 2 * lax.rem(iota(weave.shape, 0), LANES) + iota(weave.shape, 0) // LANES
        )
        keys = (offset[...] * LEAVES + target[...]).astype(F32).astype(BF16)
        item = iota((keys.shape[1], 16 * n_row), 0)
        place_at = iota((keys.shape[1], 16 * n_row), 1)
        repeat = one_hot(
            (item // SEND == place_at // 16) & (lax.rem(item, SEND) == lax.rem(place_at, SEND))
        )
        spread_keys = dot(jnp.broadcast_to(keys, (8, keys.shape[1])), repeat)[0:1]
        strip = lax.rem(iota(spread_keys.shape, 1), 16) // SEND
        hits = spread_keys.astype(jnp.int32) + strip * (OFFSETS * LEAVES)
        item_iota = iota((16, 16 * n_row), 0)
        src_rows = item_sel.shape[0]
        for i in range(src_rows // 16):
            item_sel[i * 16 : (i + 1) * 16, :] = one_hot(item_iota + i * 16 == hits)
    with scope("source_table"):
        e_iota = iota((2 * fields, source_sel.shape[1]), 1)
        e_rows = iota(e_iota.shape, 0)
        e_group = lax.rem(e_iota // (2 * full) + grp, 2)
        e_field = e_group * n_col + e_iota // (4 * full)
        e_own = e_field + lax.rem(e_iota // full, 2) * fields == e_rows
        e_block = lax.rem(e_iota, full)
        for t in range(slots):
            source_sel[t * 2 * fields : (t + 1) * 2 * fields, :] = one_hot(
                e_own & (e_block == sources[t])
            )
        for b in range(blocks):
            field_sel[b * 2 * fields : (b + 1) * 2 * fields, :] = one_hot(e_own & (e_block == b))

    cross_one = near_sum(0)
    far_local(0)
    far_image()
    image(0, cross_one)

    with scope("halo_send"):
        vec_send = send(vec.at[1], vec_cross, 4, (other, row, col))
        for x in range(2):
            last = vec[1, x * blocks + blocks - 2 : (x + 1) * blocks, :]
            halo_out[0, x * 2 : x * 2 + 2, :] = last
            halo_out[1, x * 2 : x * 2 + 2, :] = vec[1, x * blocks : x * blocks + 2, :]
        halo_two = [
            send(halo_out.at[0], halo_in.at[0, 0], 5, (grp, up, col)),
            send(halo_out.at[1], halo_in.at[0, 1], 6, (grp, down, col)),
            send(halo_out.at[0], halo_in.at[1, 0], 7, (other, up, col)),
            send(halo_out.at[1], halo_in.at[1, 1], 8, (other, down, col)),
        ]
        weigh(1)
    far_multi(1)
    with scope("vec_wait"):
        vec_send.wait_recv()
        for copy in halo_two:
            copy.wait_recv()
    with scope("extend"):
        for f in range(2):
            for x in range(2):
                lines = (vec[1] if f == 0 else vec_cross[...])[x * blocks : (x + 1) * blocks]
                ext_wide[f, x * full : x * full + blocks, :] = lines
                for side in range(2):
                    start = x * full + blocks + 2 * side
                    ext_wide[f, start : start + 2, :] = halo_in[f, side, x * 2 : x * 2 + 2, :]
        for f in range(2):
            ext_out[0, f], ext_out[1, f] = split(ext_wide[f])
        for i in range(2):
            ext_in[i, col] = ext_out[i]

    def post_ext(i):
        def post(k, carry):
            to = lax.rem(col + k, n_col)
            send_many(ext_out.at[i], ext_in.at[i, col], 4 + i, (grp, row, to))
            return carry

        lax.fori_loop(1, n_col, post, 0)

    def blocks_in(i):
        return jnp.concatenate([ext_in[i, c, f] for c in range(n_col) for f in range(2)], axis=0)

    post_ext(0)
    far_post(1)
    with scope("ext_wait"):
        await_many(ext_in.at[0, pl.ds(0, n_col - 1)], 4)
    with scope("source"):
        chosen_blocks = dot(source_sel[...], blocks_in(0)).astype(BF16)
        for t in range(slots):
            src[t] = chosen_blocks[t * 2 * fields : (t + 1) * 2 * fields]
    near_send(1)
    post_ext(1)
    far_local(1)
    cross_two = near_sum(1)
    far_image()
    image(1, cross_two)

    with scope("gram"):
        lane = iota((1, LANES), 1)
        v = [vec[i] for i in range(3)]
        turned = [
            jnp.concatenate([vec[i, blocks:, :], -vec[i, 0:blocks, :]], axis=0) for i in range(3)
        ]
        products = [
            v[0] * v[0],
            v[0] * v[1],
            v[0] * turned[1],
            v[0] * v[2],
            v[0] * turned[2],
            v[1] * v[1],
            v[1] * v[2],
            v[1] * turned[2],
            v[2] * v[2],
        ]
        packed = jnp.zeros((1, LANES), F32)
        for i, product in enumerate(products):
            total = jnp.sum(jnp.sum(product, axis=0, keepdims=True), axis=1, keepdims=True)
            packed = jnp.where(lane == i, total, packed)
        gram_out[...] = packed
        gram_in[along] = packed

    def post_gram(k, carry):
        to = lax.rem(along + k, n_grp * depth_z)
        place_to = (to // depth_z, row_of(beside, lax.rem(to, depth_z)), col)
        send_many(gram_out, gram_in.at[along], 6, place_to)
        return carry

    sides = 2 * chips
    with scope("gram_send"):
        lax.fori_loop(1, n_grp * depth_z, post_gram, 0)
    with scope("spread"):
        await_many(ext_in.at[1, pl.ds(0, n_col - 1)], 5)
        all_fields = dot(field_sel[...], blocks_in(0)) + dot(field_sel[...], blocks_in(1))
        for b in range(blocks):
            for x in range(2):
                start = (b * 2 + x) * fields
                spread[x, :, b * TILE : (b + 1) * TILE] = all_fields[start : start + fields]
    with scope("gram_wait"):
        await_many(gram_in.at[pl.ds(0, n_grp * depth_z - 1)], 6)
        for i in range(n_grp):
            cross_out[i] = jnp.sum(gram_in[i * depth_z : (i + 1) * depth_z], axis=0)
        cross_in[beside] = cross_out[...]

    def post_cross(k, carry):
        to = (grp, row_of(lax.rem(beside + k, sides), lax.rem(row // 2, depth_z)), col)
        send_many(cross_out, cross_in.at[beside], 7, to)
        return carry

    lax.fori_loop(1, sides, post_cross, 0)
    with scope("cross_gram_wait"):
        await_many(cross_in.at[pl.ds(0, sides - 1)], 7)
    with scope("solve"):
        total = jnp.sum(cross_in[...], axis=0)
        total = jnp.concatenate([total[0], total[1]], axis=0)
        lane = iota((2, LANES), 1)
        g = [jnp.sum(jnp.where(lane == i, total, 0.0), axis=1, keepdims=True) for i in range(9)]
        alpha, gamma = solve(g[0], (g[1], g[2]), (g[3], g[4]), g[5], (g[6], g[7]), g[8])
        packed = jnp.zeros((2, LANES), F32)
        for i, value in enumerate((*alpha, *gamma)):
            packed = jnp.where(lane == i, value, packed)
        for i in range(n_grp):
            coef_out[i] = packed[i : i + 1]
        coef_in[col] = coef_out[...]

    def post_coef(k, carry):
        send_many(coef_out, coef_in.at[col], 8, (grp, row, lax.rem(col + k, n_col)))
        return carry

    lax.fori_loop(1, n_col, post_coef, 0)
    with scope("coef_wait"):
        await_many(coef_in.at[pl.ds(0, n_col - 1)], 8)
    with scope("combine"):
        for i in range(n_grp):
            for j in range(n_col):
                coef[i * n_col + j : i * n_col + j + 1, :] = coef_in[j, i]
        c = [coef[:, i : i + 1] for i in range(4)]
        for b in range(blocks):
            at = slice(b * TILE, (b + 1) * TILE)
            b0, b1, f0, f1 = rhs[0, :, at], rhs[1, :, at], spread[0, :, at], spread[1, :, at]
            out[0, :, at] = c[0] * b0 - c[1] * b1 + c[2] * f0 - c[3] * f1
            out[1, :, at] = c[0] * b1 + c[1] * b0 + c[2] * f1 + c[3] * f0

    with scope("sent_wait"):
        for copy in (*halo_one, cross_one, vec_send, *halo_two, cross_two):
            copy.wait_send()
        for step in range(2):
            await_sent(multi_in.at[step, pl.ds(0, (n_row - 1) * 16)], step)
            await_sent(near_in.at[step, pl.ds(0, n_col - 1)], 2 + step)
            await_sent(ext_in.at[step, pl.ds(0, n_col - 1)], 4 + step)
        await_sent(gram_in.at[pl.ds(0, n_grp * depth_z - 1)], 6)
        await_sent(cross_in.at[pl.ds(0, sides - 1)], 7)
        await_sent(coef_in.at[pl.ds(0, n_col - 1)], 8)


def local_part(
    right_side,
    near_tiles,
    tile_pairs,
    tile_count,
    panel_expansions,
    leaf_of_panel,
    far_pick,
    far_target,
    far_offset,
    translations,
):
    n_grp, n_row, n_col = (lax.axis_size(axis) for axis in ("grp", "row", "col"))
    fields, panels = right_side.shape[1:]
    blocks = panels // TILE
    slots = near_tiles.shape[1]
    coefs = panel_expansions.shape[2]
    parts = pl.cdiv(coefs, LANES)
    strips = pl.cdiv(2 * coefs, LANES)
    exps = jnp.transpose(panel_expansions, (2, 0, 1))
    trans = jnp.transpose(translations, (0, 2, 1, 3))
    whole_part = (parts - 1) * LANES
    spare = [(0, 0, 0)] * 3 + [(-whole_part, parts * LANES - coefs, 0)]
    tail = lax.pad(trans, jnp.zeros((), BF16), spare)
    full = blocks + 2 * REACH
    rows = 2 * blocks
    depth = n_col * 4 * full
    vm = pltpu.VMEM
    scratch = [
        vm(right_side.shape, F32),
        vm(near_tiles.shape, BF16),
        vm((panels // LANES, coefs, 2, LANES), BF16),
        vm((parts, OFFSETS, coefs, 2, LANES), BF16),
        vm((n_row, SEND, LANES), F32),
        vm((16 * n_row, TILE), BF16),
        vm((strips * OFFSETS * LEAVES, 16 * n_row), BF16),
        vm((TILE, TILE), BF16),
        vm((n_col * n_grp * rows, 4 * slots * fields), BF16),
        vm((slots * 2 * fields, depth), BF16),
        vm((blocks * 2 * fields, depth), BF16),
        vm((3, rows, TILE), F32),
        vm((rows, TILE), F32),
        vm((2 * LEAVES, panels), BF16),
        vm((2 * LEAVES, strips * LANES), F32),
        vm((TILE, LANES), F32),
        vm((2, 16 * n_row, LANES), BF16),
        vm((2, 16 * n_row, LANES), BF16),
        vm((4 * LEAVES, strips * LANES), BF16),
        vm((2 * LEAVES, strips * LANES), F32),
        vm((4 * LEAVES, parts * TILE), BF16),
        vm((full, 2 * fields, TILE), BF16),
        vm((slots, 2 * fields, TILE), BF16),
        vm((4 * slots * fields, TILE), BF16),
        vm((2, n_col, n_grp * rows, TILE), BF16),
        vm((2, n_col, n_grp * rows, TILE), BF16),
        vm((2, n_grp * rows, TILE), F32),
        vm((2, rows, TILE), F32),
        vm((2, 8, TILE), F32),
        vm((2, 2, 8, TILE), F32),
        vm((rows, TILE), F32),
        vm((2, 2 * full, TILE), F32),
        vm((2, 2, 2 * full, TILE), BF16),
        vm((2, n_col, 2, 2 * full, TILE), BF16),
        vm(right_side.shape, F32),
        vm((fields, LANES), F32),
        vm((1, LANES), F32),
        vm((n_grp * 6, 1, LANES), F32),
        vm((n_grp, 1, LANES), F32),
        vm((n_row // 6, n_grp, 1, LANES), F32),
        vm((n_grp, 1, LANES), F32),
        vm((n_col, n_grp, 1, LANES), F32),
        pltpu.SemaphoreType.DMA((4,)),
        pltpu.SemaphoreType.DMA((9,)),
        pltpu.SemaphoreType.DMA((9,)),
        pltpu.SemaphoreType.DMA((9,)),
        pltpu.SemaphoreType.DMA((9,)),
    ]
    smem = pl.BlockSpec(memory_space=pltpu.SMEM)
    whole = pl.BlockSpec(memory_space=pltpu.VMEM)
    hbm = pl.BlockSpec(memory_space=pl.ANY)
    sizes = (n_grp, n_row, n_col, fields, blocks, slots, coefs)
    return pl.pallas_call(
        functools.partial(kernel, sizes),
        out_shape=jax.ShapeDtypeStruct(right_side.shape, F32),
        in_specs=[smem, smem, whole, whole, whole, whole, hbm, hbm, hbm, hbm, hbm],
        out_specs=whole,
        scratch_shapes=scratch,
        compiler_params=pltpu.CompilerParams(
            collective_id=0, has_side_effects=True, vmem_limit_bytes=60 << 20
        ),
    )(
        tile_pairs,
        tile_count,
        jnp.transpose(far_pick, (0, 2, 1)),
        leaf_of_panel,
        far_target,
        far_offset,
        right_side,
        near_tiles,
        exps,
        trans,
        tail,
    )


def solution(mesh):
    return jax.shard_map(
        local_part,
        mesh=mesh,
        in_specs=(
            P(None, None, "row"),
            P(None, ("grp", "row", "col"), None, None),
            P(("grp", "row", "col")),
            P(("grp", "row", "col")),
            P(None, "row", None),
            P("row", None),
            P(),
            P("row", None),
            P("row", None),
            P(),
        ),
        out_specs=P(None, None, "row"),
        check_vma=False,
    )
```

```python
import functools

import jax
import jax.numpy as jnp
from jax import lax
from jax.experimental import pallas as pl
from jax.experimental.pallas import tpu as pltpu
from jax.sharding import PartitionSpec as P

REACH = 2
SPAN = 2 * REACH + 1
OFFSETS = 4
LEAVES = 24
SEND = 2
TILE = 256
LANES = 128
EPSILON = 1e-06
MESH = pl.DeviceIdType.MESH
F32 = jnp.float32
BF16 = jnp.bfloat16


def dot(a, b):
    return jnp.dot(a, b, preferred_element_type=F32)


def dot_nt(a, b):
    return lax.dot_general(a, b, (((1,), (1,)), ((), ())), preferred_element_type=F32)


def iota(shape, dim):
    return lax.broadcasted_iota(jnp.int32, shape, dim)


def one_hot(condition):
    return jnp.where(condition, 1.0, 0.0).astype(BF16)


def c_mul(a, b):
    return (a[0] * b[0] - a[1] * b[1], a[0] * b[1] + a[1] * b[0])


def c_add(a, b):
    return (a[0] + b[0], a[1] + b[1])


def c_scale(a, s):
    return (a[0] * s, a[1] * s)


def c_conj(a):
    return (a[0], -a[1])


def c_square(a):
    return a[0] * a[0] + a[1] * a[1]


def solve(bb, bf, bg, ff, fg, gg):
    beta = jnp.sqrt(bb + EPSILON)
    inv = 1.0 / beta
    inv2 = inv * inv
    bb, ff, gg = bb * inv2, ff * inv2, gg * inv2
    bf, bg, fg = c_scale(bf, inv2), c_scale(bg, inv2), c_scale(fg, inv2)
    h11 = (0.5 * bb + bf[0], bf[1])
    a = (0.5 - h11[0], -h11[1])
    u_square = ff + 2.0 * c_mul(c_conj(a), bf)[0] + c_square(a) * bb
    h21 = jnp.sqrt(jnp.maximum(u_square, 0.0) + EPSILON)
    inv21 = 1.0 / h21
    p = (a[0] + 0.5, a[1])
    q = c_scale(a, 0.5)
    x_b = c_add(c_add(bg, c_mul(p, bf)), c_scale(q, bb))
    x_f = c_add(c_add(fg, c_scale(p, ff)), c_mul(q, c_conj(bf)))
    h12 = c_scale(x_b, inv21)
    h22 = c_scale(c_add(x_f, c_mul(c_conj(a), x_b)), inv21 * inv21)
    p2 = (p[0] - h22[0], p[1] - h22[1])
    ha = c_mul(h22, a)
    q2 = (q[0] - x_b[0] - ha[0], q[1] - x_b[1] - ha[1])
    r_square = (
        gg
        + c_square(p2) * ff
        + c_square(q2) * bb
        + 2.0 * c_mul(p2, c_conj(fg))[0]
        + 2.0 * c_mul(q2, c_conj(bg))[0]
        + 2.0 * c_mul(c_mul(c_conj(p2), q2), c_conj(bf))[0]
    ) * (inv21 * inv21)
    h32 = jnp.sqrt(jnp.maximum(r_square, 0.0) + EPSILON)
    rho1 = jnp.sqrt(c_square(h11) + h21 * h21)
    c1 = c_scale(h11, 1.0 / rho1)
    s1 = h21 / rho1
    r12 = c_add(c_mul(c_conj(c1), h12), c_scale(h22, s1))
    t = c_add(c_mul(c1, h22), c_scale(h12, -s1))
    rho2 = jnp.sqrt(c_square(t) + h32 * h32)
    c2 = c_scale(t, 1.0 / rho2)
    y2 = c_scale(c_conj(c2), -s1 * beta / rho2)
    y1 = c_add(c_scale(c_conj(c1), beta), c_scale(c_mul(r12, y2), -1.0))
    y1 = c_scale(y1, 1.0 / rho1)
    y2 = c_scale(y2, inv21)
    alpha = c_scale(c_add(y1, c_mul(y2, a)), inv)
    return alpha, c_scale(y2, inv)


def kernel(
    sizes,
    pairs,
    count,
    pick,
    leaf,
    target,
    offset,
    rhs_hbm,
    tiles_hbm,
    exps_hbm,
    trans_hbm,
    tail_hbm,
    out_b,
    out_f,
    rhs,
    tiles,
    exps,
    trans,
    pick_rows,
    pick_sel,
    item_sel,
    weave,
    place,
    source_sel,
    field_sel,
    vec,
    far,
    weighted,
    multi_wide,
    multi,
    multi_out,
    multi_in,
    gathered,
    local,
    woven,
    ext_one,
    src,
    values,
    near_out,
    near_in,
    near_part,
    near_cross,
    halo_out,
    halo_in,
    vec_cross,
    ext_wide,
    ext_out,
    ext_in,
    spread,
    coef,
    gram_out,
    gram_in,
    cross_out,
    cross_in,
    coef_out,
    coef_in,
    load_sem,
    send_sem,
    recv_sem,
    many_send,
    many_recv,
):
    n_grp, n_row, n_col, fields, blocks, slots, coefs = sizes
    grp, row, col = lax.axis_index("grp"), lax.axis_index("row"), lax.axis_index("col")
    other = 1 - grp
    mine = grp * n_col + col
    chips, depth_z = n_row // 12, 6
    along = grp * depth_z + lax.rem(row // 2, depth_z)
    beside = (row // (2 * depth_z)) * 2 + lax.rem(row, 2)
    up, down = lax.rem(row + 1, n_row), lax.rem(row + n_row - 1, n_row)
    full = blocks + 2 * REACH
    rows = 2 * blocks
    pairs_wide = 2 * coefs
    wide = multi_wide.shape[1]
    strips = wide // LANES
    scope = jax.named_scope

    pltpu.make_async_copy(rhs_hbm, rhs, load_sem.at[0]).start()
    for i in range(rows):
        pltpu.make_async_copy(
            exps_hbm.at[:, :, pl.ds(i * LANES, LANES)], exps.at[i], load_sem.at[1]
        ).start()
    pltpu.make_async_copy(tiles_hbm, tiles, load_sem.at[2]).start()
    parts = trans.shape[0]
    for i in range(parts):
        piece = tail_hbm if i == parts - 1 else trans_hbm.at[:, :, :, pl.ds(i * LANES, LANES)]
        pltpu.make_async_copy(piece, trans.at[i], load_sem.at[3]).start()

    def loaded(ref, sem):
        pltpu.make_async_copy(ref, ref, load_sem.at[sem]).wait()

    barrier = pltpu.get_barrier_semaphore()

    def greet(to):
        pl.semaphore_signal(barrier, inc=1, device_id=to, device_id_type=MESH)

    def greet_row(k, carry):
        greet((grp, lax.rem(row + k, n_row), col))
        return carry

    def greet_col(k, carry):
        greet((grp, row, lax.rem(col + k, n_col)))
        return carry

    def row_of(side, z):
        return (side // 2) * (2 * depth_z) + z * 2 + lax.rem(side, 2)

    def greet_other(z, carry):
        greet((other, row_of(beside, z), col))
        return carry

    with scope("greet"):
        lax.fori_loop(1, n_row, greet_row, 0)
        lax.fori_loop(0, depth_z, greet_other, 0)
        lax.fori_loop(1, n_col, greet_col, 0)
        greet((other, up, col))
        greet((other, down, col))

    def send(source, target, sem, to):
        copy = pltpu.make_async_remote_copy(
            src_ref=source,
            dst_ref=target,
            send_sem=send_sem.at[sem],
            recv_sem=recv_sem.at[sem],
            device_id=to,
            device_id_type=MESH,
        )
        copy.start()
        return copy

    def send_many(source, target, sem, to):
        pltpu.make_async_remote_copy(
            src_ref=source,
            dst_ref=target,
            send_sem=many_send.at[sem],
            recv_sem=many_recv.at[sem],
            device_id=to,
            device_id_type=MESH,
        ).start()

    def await_many(ref, sem):
        pltpu.make_async_copy(ref, ref, many_recv.at[sem]).wait()

    def await_sent(ref, sem):
        pltpu.make_async_copy(ref, ref, many_send.at[sem]).wait()

    with scope("right_side"):
        loaded(rhs, 0)
        for x in range(2):
            for b in range(blocks):
                vec[0, x * blocks + b : x * blocks + b + 1, :] = rhs[
                    x, pl.ds(mine, 1), b * TILE : (b + 1) * TILE
                ]
        for b in range(blocks):
            for x in range(2):
                ext_one[b, x * fields : (x + 1) * fields, :] = rhs[
                    x, :, b * TILE : (b + 1) * TILE
                ].astype(BF16)

    def member(b):
        return iota((LEAVES, TILE), 0) == leaf[:, b * TILE : (b + 1) * TILE]

    def weigh(step):
        for b in range(blocks):
            inside = member(b)
            for x in range(2):
                line = vec[step, x * blocks + b : x * blocks + b + 1, :]
                weighted[x * LEAVES : (x + 1) * LEAVES, b * TILE : (b + 1) * TILE] = jnp.where(
                    inside, line, 0.0
                ).astype(BF16)

    with scope("pick_table"):
        multi_wide[...] = jnp.zeros_like(multi_wide)
        multi[...] = jnp.zeros_like(multi)
        halo_out[...] = jnp.zeros_like(halo_out)
        here_lane = iota(pick.shape, 2) == row
        chosen = jnp.sum(jnp.where(here_lane, pick[...].astype(F32), 0.0), axis=2, keepdims=True)
        pick_rows[...] = jnp.broadcast_to(chosen, pick_rows.shape)
        rows16, lanes16 = iota((16, LANES), 0), iota((16, LANES), 1)
        even16 = lax.rem(rows16, 2) == 0
        base16 = jnp.where(rows16 < 2 * strips, (rows16 // 2) * LEAVES, 2 * TILE)

        def build_pick(d, carry):
            own = pick_rows[d].astype(jnp.int32)
            hit = base16 + jnp.where(even16, own[0:1], own[1:2])
            at = pl.ds(pl.multiple_of(d * 16, 16), 16)
            pick_sel[at, 0:LANES] = one_hot(lanes16 == hit)
            pick_sel[at, LANES:] = one_hot(lanes16 + LANES == hit)
            return carry

        lax.fori_loop(0, n_row, build_pick, 0)
    with scope("weigh"):
        weigh(0)
    panels_of = exps.reshape(rows, pairs_wide, LANES)

    def panel_block(b):
        return jnp.concatenate([panels_of[2 * b], panels_of[2 * b + 1]], axis=1)

    def swapped(value):
        left = pltpu.roll(value, wide - 1, 1)
        right = pltpu.roll(value, 1, 1)
        return left, right

    lane_even = lax.rem(iota((LEAVES, wide), 1), 2) == 0

    here = pl.ds(pl.multiple_of(row * 16, 16), 16)

    def far_multi(step):
        with scope("multi"):
            total = None
            for b in range(blocks):
                term = dot_nt(weighted[:, b * TILE : (b + 1) * TILE], panel_block(b))
                total = term if total is None else total + term
            multi_wide[:, 0:pairs_wide] = total
            left, right = swapped(multi_wide[LEAVES:, :])
            total = multi_wide[0:LEAVES, :] + jnp.where(lane_even, -left, right)
            for i in range(strips):
                multi[i * LEAVES : (i + 1) * LEAVES, :] = total[:, i * LANES : (i + 1) * LANES]
            multi_out[step] = dot(pick_sel[...], multi[...].astype(BF16)).astype(BF16)
            multi_in[step, here, :] = multi_out[step, here, :]

    def far_post(step):
        def post(k, carry):
            to = lax.rem(row + 1 + lax.rem(k + n_row // 3, n_row - 1), n_row)
            send_many(
                multi_out.at[step, pl.ds(pl.multiple_of(to * 16, 16), 16)],
                multi_in.at[step, here],
                step,
                (grp, to, col),
            )
            return carry

        with scope("multi_send"):
            lax.fori_loop(0, n_row - 1, post, 0)

    def split(value):
        high = value.astype(BF16)
        return high, (value - high.astype(F32)).astype(BF16)

    def far_local(step):
        with scope("multi_wait"):
            await_many(multi_in.at[step, pl.ds(0, (n_row - 1) * 16)], step)
        if step == 0:
            loaded(trans, 3)
        with scope("translate"):
            picked = dot(item_sel[...], multi_in[step])
            pieces = trans.reshape(parts, OFFSETS, pairs_wide, LANES)
            total = None
            for o in range(OFFSETS):
                lines = jnp.concatenate(
                    [
                        picked[(i * OFFSETS + o) * LEAVES : (i * OFFSETS + o + 1) * LEAVES]
                        for i in range(strips)
                    ],
                    axis=1,
                )
                left, right = swapped(lines)
                for x, value in enumerate(
                    (jnp.where(lane_even, lines, -lines), jnp.where(lane_even, left, right))
                ):
                    local[x * LEAVES : (x + 1) * LEAVES, :] = value
                high, low = split(local[...])
                gathered[0 : 2 * LEAVES, :] = high
                gathered[2 * LEAVES :, :] = low
                matrix = jnp.concatenate([pieces[i, o] for i in range(parts)], axis=1)
                term = dot(gathered[:, 0:pairs_wide], matrix)
                total = term if total is None else total + term
            field = total[0 : 2 * LEAVES] + total[2 * LEAVES :]
            real, imag = field[0:LEAVES], field[LEAVES:]
            stacked = []
            for i in range(parts):
                r, m = (v[:, i * LANES : (i + 1) * LANES] for v in (real, imag))
                lines = jnp.concatenate(
                    [jnp.concatenate([r, -m], axis=1), jnp.concatenate([m, r], axis=1)], axis=0
                )
                stacked.extend(split(lines))
            mixed = dot(jnp.concatenate(stacked, axis=0), weave[...]).astype(BF16)
            for i in range(parts):
                woven[:, i * TILE : (i + 1) * TILE] = mixed[
                    i * 4 * LEAVES : (i + 1) * 4 * LEAVES
                ]

    def far_image():
        with scope("evaluate"):
            lines = woven[:, 0:pairs_wide]
            for b in range(blocks):
                found = dot(lines, panel_block(b))
                found = found[0 : 2 * LEAVES] + found[2 * LEAVES :]
                inside = member(b)
                for x in range(2):
                    value = jnp.where(inside, found[x * LEAVES : (x + 1) * LEAVES], 0.0)
                    at = x * blocks + b
                    far[at : at + 1, :] = jnp.sum(value, axis=0, keepdims=True)

    def near_send(step):
        with scope("near"):
            for t in range(slots):
                by_real = dot_nt(src[t], tiles[0, t])
                by_imag = dot_nt(src[t], tiles[1, t])
                real = by_real[0:fields] - by_imag[fields:]
                imag = by_imag[0:fields] + by_real[fields:]
                for x, value in enumerate((real, imag)):
                    start = (x * slots + t) * fields
                    high, low = split(value)
                    values[start : start + fields, :] = high
                    values[half + start : half + start + fields, :] = low
            image = dot(place[...], values[...]).astype(BF16)
            for c in range(n_col):
                near_out[step, c] = image[c * width : (c + 1) * width]
            near_in[step, col] = near_out[step, col]

        def post(k, carry):
            to = lax.rem(col + k, n_col)
            send_many(near_out.at[step, to], near_in.at[step, col], 2 + step, (grp, row, to))
            return carry

        with scope("near_send"):
            lax.fori_loop(1, n_col, post, 0)

    def near_sum(step):
        with scope("near_wait"):
            await_many(near_in.at[step, pl.ds(0, n_col - 1)], 2 + step)
        with scope("near_sum"):
            near_part[step] = jnp.sum(near_in[step].astype(F32), axis=0)
            start = pl.multiple_of(other * rows, 8)
            return send(
                near_part.at[step, pl.ds(start, rows)],
                near_cross.at[step],
                2 + step,
                (other, row, col),
            )

    def image(step, cross):
        with scope("cross_wait"):
            cross.wait_recv()
        start = pl.multiple_of(grp * rows, 8)
        vec[step + 1] = near_part[step, pl.ds(start, rows), :] + near_cross[step] + far[...]

    with scope("exps_wait"):
        loaded(exps, 1)
    far_multi(0)
    with scope("barrier_wait"):
        pl.semaphore_wait(barrier, (n_row - 1) + depth_z + (n_col - 1) + 2)
    halo_one = [
        send(ext_one.at[pl.ds(blocks - 2, 2)], ext_one.at[pl.ds(blocks, 2)], 0, (grp, up, col)),
        send(ext_one.at[pl.ds(0, 2)], ext_one.at[pl.ds(blocks + 2, 2)], 1, (grp, down, col)),
    ]
    far_post(0)

    with scope("near_table"):
        targets = [pairs[t] // SPAN for t in range(slots)]
        sources = []
        for t in range(slots):
            rel = targets[t] + lax.rem(pairs[t], SPAN) - REACH
            inner = jnp.where(rel >= blocks, rel + REACH, rel)
            sources.append(jnp.where(rel < 0, rel + blocks + REACH, inner))
        half = 2 * slots * fields
        k_iota = iota((1, 2 * half), 1)
        k_slot = lax.rem(k_iota, slots * fields) // fields
        k_field = lax.rem(k_iota, fields)
        k_part = lax.rem(k_iota, half) // (slots * fields)
        k_target = jnp.full_like(k_iota, -1)
        for t in range(slots):
            goal = jnp.where(t < count[0], targets[t], -1)
            k_target = jnp.where(k_slot == t, goal, k_target)
        width = n_grp * rows
        k_row = lax.rem(k_field, n_col) * width + (k_field // n_col) * rows + k_part * blocks
        k_row = jnp.where(k_target < 0, -1, k_row + k_target)
        place[...] = one_hot(iota(place.shape, 0) == k_row)
    with scope("halo_wait"):
        loaded(tiles, 2)
        for copy in halo_one:
            copy.wait_recv()
    for t in range(slots):
        src[t] = ext_one[sources[t]]
    near_send(0)
    with scope("item_table"):
        weave[...] = one_hot(
            iota(weave.shape, 1)
            == 2 * lax.rem(iota(weave.shape, 0), LANES) + iota(weave.shape, 0) // LANES
        )
        keys = (offset[...] * LEAVES + target[...]).astype(F32).astype(BF16)
        item = iota((keys.shape[1], 16 * n_row), 0)
        place_at = iota((keys.shape[1], 16 * n_row), 1)
        repeat = one_hot(
            (item // SEND == place_at // 16) & (lax.rem(item, SEND) == lax.rem(place_at, SEND))
        )
        spread_keys = dot(jnp.broadcast_to(keys, (8, keys.shape[1])), repeat)[0:1]
        strip = lax.rem(iota(spread_keys.shape, 1), 16) // SEND
        hits = spread_keys.astype(jnp.int32) + strip * (OFFSETS * LEAVES)
        item_iota = iota((16, 16 * n_row), 0)
        src_rows = item_sel.shape[0]
        for i in range(src_rows // 16):
            item_sel[i * 16 : (i + 1) * 16, :] = one_hot(item_iota + i * 16 == hits)
    with scope("source_table"):
        e_iota = iota((2 * fields, source_sel.shape[1]), 1)
        e_rows = iota(e_iota.shape, 0)
        e_group = lax.rem(e_iota // (2 * full) + grp, 2)
        e_field = e_group * n_col + e_iota // (4 * full)
        e_own = e_field + lax.rem(e_iota // full, 2) * fields == e_rows
        e_block = lax.rem(e_iota, full)
        for t in range(slots):
            source_sel[t * 2 * fields : (t + 1) * 2 * fields, :] = one_hot(
                e_own & (e_block == sources[t])
            )
        for b in range(blocks):
            field_sel[b * 2 * fields : (b + 1) * 2 * fields, :] = one_hot(e_own & (e_block == b))

    cross_one = near_sum(0)
    far_local(0)
    far_image()
    image(0, cross_one)

    with scope("halo_send"):
        vec_send = send(vec.at[1], vec_cross, 4, (other, row, col))
        for x in range(2):
            last = vec[1, x * blocks + blocks - 2 : (x + 1) * blocks, :]
            halo_out[0, x * 2 : x * 2 + 2, :] = last
            halo_out[1, x * 2 : x * 2 + 2, :] = vec[1, x * blocks : x * blocks + 2, :]
        halo_two = [
            send(halo_out.at[0], halo_in.at[0, 0], 5, (grp, up, col)),
            send(halo_out.at[1], halo_in.at[0, 1], 6, (grp, down, col)),
            send(halo_out.at[0], halo_in.at[1, 0], 7, (other, up, col)),
            send(halo_out.at[1], halo_in.at[1, 1], 8, (other, down, col)),
        ]
        weigh(1)

    def extend(f):
        for x in range(2):
            lines = (vec[1] if f == 0 else vec_cross[...])[x * blocks : (x + 1) * blocks]
            ext_wide[f, x * full : x * full + blocks, :] = lines
            for side in range(2):
                start = x * full + blocks + 2 * side
                ext_wide[f, start : start + 2, :] = halo_in[f, side, x * 2 : x * 2 + 2, :]
        ext_out[0, f], ext_out[1, f] = split(ext_wide[f])
        for i in range(2):
            ext_in[i, col, f] = ext_out[i, f]

    def post_ext(i, f):
        def post(k, carry):
            to = lax.rem(col + k, n_col)
            send_many(ext_out.at[i, f], ext_in.at[i, col, f], 4 + i, (grp, row, to))
            return carry

        lax.fori_loop(1, n_col, post, 0)

    def blocks_in(i):
        return jnp.concatenate([ext_in[i, c, f] for c in range(n_col) for f in range(2)], axis=0)

    with scope("extend_own"):
        for copy in halo_two[:2]:
            copy.wait_recv()
        extend(0)
        post_ext(0, 0)
    far_multi(1)
    with scope("extend_other"):
        vec_send.wait_recv()
        for copy in halo_two[2:]:
            copy.wait_recv()
        extend(1)
        post_ext(0, 1)
    far_post(1)
    with scope("ext_wait"):
        await_many(ext_in.at[0, pl.ds(0, n_col - 1)], 4)
    with scope("source"):
        chosen_blocks = dot(source_sel[...], blocks_in(0)).astype(BF16)
        for t in range(slots):
            src[t] = chosen_blocks[t * 2 * fields : (t + 1) * 2 * fields]
    near_send(1)
    far_local(1)
    cross_two = near_sum(1)
    for f in range(2):
        post_ext(1, f)
    far_image()
    image(1, cross_two)

    with scope("gram"):
        lane = iota((1, LANES), 1)
        v = [vec[i] for i in range(3)]
        turned = [
            jnp.concatenate([vec[i, blocks:, :], -vec[i, 0:blocks, :]], axis=0) for i in range(3)
        ]
        products = [
            v[0] * v[0],
            v[0] * v[1],
            v[0] * turned[1],
            v[0] * v[2],
            v[0] * turned[2],
            v[1] * v[1],
            v[1] * v[2],
            v[1] * turned[2],
            v[2] * v[2],
        ]
        packed = jnp.zeros((1, LANES), F32)
        for i, product in enumerate(products):
            total = jnp.sum(jnp.sum(product, axis=0, keepdims=True), axis=1, keepdims=True)
            packed = jnp.where(lane == i, total, packed)
        gram_out[...] = packed
        gram_in[along] = packed

    def post_gram(k, carry):
        to = lax.rem(along + k, n_grp * depth_z)
        place_to = (to // depth_z, row_of(beside, lax.rem(to, depth_z)), col)
        send_many(gram_out, gram_in.at[along], 6, place_to)
        return carry

    sides = 2 * chips
    with scope("gram_send"):
        lax.fori_loop(1, n_grp * depth_z, post_gram, 0)
    with scope("spread"):
        await_many(ext_in.at[1, pl.ds(0, n_col - 1)], 5)
        all_fields = dot(field_sel[...], blocks_in(0)) + dot(field_sel[...], blocks_in(1))
        for b in range(blocks):
            for x in range(2):
                start = (b * 2 + x) * fields
                spread[x, :, b * TILE : (b + 1) * TILE] = all_fields[start : start + fields]
    with scope("gram_wait"):
        await_many(gram_in.at[pl.ds(0, n_grp * depth_z - 1)], 6)
        for i in range(n_grp):
            cross_out[i] = jnp.sum(gram_in[i * depth_z : (i + 1) * depth_z], axis=0)
        cross_in[beside] = cross_out[...]

    def post_cross(k, carry):
        to = (grp, row_of(lax.rem(beside + k, sides), lax.rem(row // 2, depth_z)), col)
        send_many(cross_out, cross_in.at[beside], 7, to)
        return carry

    lax.fori_loop(1, sides, post_cross, 0)
    with scope("cross_gram_wait"):
        await_many(cross_in.at[pl.ds(0, sides - 1)], 7)
    with scope("solve"):
        total = jnp.sum(cross_in[...], axis=0)
        total = jnp.concatenate([total[0], total[1]], axis=0)
        lane = iota((2, LANES), 1)
        g = [jnp.sum(jnp.where(lane == i, total, 0.0), axis=1, keepdims=True) for i in range(9)]
        alpha, gamma = solve(g[0], (g[1], g[2]), (g[3], g[4]), g[5], (g[6], g[7]), g[8])
        packed = jnp.zeros((2, LANES), F32)
        for i, value in enumerate((*alpha, *gamma)):
            packed = jnp.where(lane == i, value, packed)
        for i in range(n_grp):
            coef_out[i] = packed[i : i + 1]
        coef_in[col] = coef_out[...]

    def post_coef(k, carry):
        send_many(coef_out, coef_in.at[col], 8, (grp, row, lax.rem(col + k, n_col)))
        return carry

    lax.fori_loop(1, n_col, post_coef, 0)
    with scope("coef_wait"):
        await_many(coef_in.at[pl.ds(0, n_col - 1)], 8)
    with scope("combine"):
        for i in range(n_grp):
            for j in range(n_col):
                coef[i * n_col + j : i * n_col + j + 1, :] = coef_in[j, i]
        c = [coef[:, i : i + 1] for i in range(4)]
        for b in range(blocks):
            at = slice(b * TILE, (b + 1) * TILE)
            b0, b1, f0, f1 = rhs[0, :, at], rhs[1, :, at], spread[0, :, at], spread[1, :, at]
            out_b[0, :, at] = c[0] * b0 - c[1] * b1
            out_b[1, :, at] = c[0] * b1 + c[1] * b0
            out_f[0, :, at] = c[2] * f0 - c[3] * f1
            out_f[1, :, at] = c[2] * f1 + c[3] * f0

    with scope("sent_wait"):
        for copy in (*halo_one, cross_one, vec_send, *halo_two, cross_two):
            copy.wait_send()
        for step in range(2):
            await_sent(multi_in.at[step, pl.ds(0, (n_row - 1) * 16)], step)
            await_sent(near_in.at[step, pl.ds(0, n_col - 1)], 2 + step)
            await_sent(ext_in.at[step, pl.ds(0, n_col - 1)], 4 + step)
        await_sent(gram_in.at[pl.ds(0, n_grp * depth_z - 1)], 6)
        await_sent(cross_in.at[pl.ds(0, sides - 1)], 7)
        await_sent(coef_in.at[pl.ds(0, n_col - 1)], 8)


def local_part(
    right_side,
    near_tiles,
    tile_pairs,
    tile_count,
    panel_expansions,
    leaf_of_panel,
    far_pick,
    far_target,
    far_offset,
    translations,
):
    n_grp, n_row, n_col = (lax.axis_size(axis) for axis in ("grp", "row", "col"))
    fields, panels = right_side.shape[1:]
    blocks = panels // TILE
    slots = near_tiles.shape[1]
    coefs = panel_expansions.shape[2]
    parts = pl.cdiv(coefs, LANES)
    strips = pl.cdiv(2 * coefs, LANES)
    exps = jnp.transpose(panel_expansions, (2, 0, 1))
    trans = jnp.transpose(translations, (0, 2, 1, 3))
    whole_part = (parts - 1) * LANES
    spare = [(0, 0, 0)] * 3 + [(-whole_part, parts * LANES - coefs, 0)]
    tail = lax.pad(trans, jnp.zeros((), BF16), spare)
    full = blocks + 2 * REACH
    rows = 2 * blocks
    depth = n_col * 4 * full
    vm = pltpu.VMEM
    scratch = [
        vm(right_side.shape, F32),
        vm(near_tiles.shape, BF16),
        vm((panels // LANES, coefs, 2, LANES), BF16),
        vm((parts, OFFSETS, coefs, 2, LANES), BF16),
        vm((n_row, SEND, LANES), F32),
        vm((16 * n_row, TILE), BF16),
        vm((strips * OFFSETS * LEAVES, 16 * n_row), BF16),
        vm((TILE, TILE), BF16),
        vm((n_col * n_grp * rows, 4 * slots * fields), BF16),
        vm((slots * 2 * fields, depth), BF16),
        vm((blocks * 2 * fields, depth), BF16),
        vm((3, rows, TILE), F32),
        vm((rows, TILE), F32),
        vm((2 * LEAVES, panels), BF16),
        vm((2 * LEAVES, strips * LANES), F32),
        vm((TILE, LANES), F32),
        vm((2, 16 * n_row, LANES), BF16),
        vm((2, 16 * n_row, LANES), BF16),
        vm((4 * LEAVES, strips * LANES), BF16),
        vm((2 * LEAVES, strips * LANES), F32),
        vm((4 * LEAVES, parts * TILE), BF16),
        vm((full, 2 * fields, TILE), BF16),
        vm((slots, 2 * fields, TILE), BF16),
        vm((4 * slots * fields, TILE), BF16),
        vm((2, n_col, n_grp * rows, TILE), BF16),
        vm((2, n_col, n_grp * rows, TILE), BF16),
        vm((2, n_grp * rows, TILE), F32),
        vm((2, rows, TILE), F32),
        vm((2, 8, TILE), F32),
        vm((2, 2, 8, TILE), F32),
        vm((rows, TILE), F32),
        vm((2, 2 * full, TILE), F32),
        vm((2, 2, 2 * full, TILE), BF16),
        vm((2, n_col, 2, 2 * full, TILE), BF16),
        vm(right_side.shape, F32),
        vm((fields, LANES), F32),
        vm((1, LANES), F32),
        vm((n_grp * 6, 1, LANES), F32),
        vm((n_grp, 1, LANES), F32),
        vm((n_row // 6, n_grp, 1, LANES), F32),
        vm((n_grp, 1, LANES), F32),
        vm((n_col, n_grp, 1, LANES), F32),
        pltpu.SemaphoreType.DMA((4,)),
        pltpu.SemaphoreType.DMA((9,)),
        pltpu.SemaphoreType.DMA((9,)),
        pltpu.SemaphoreType.DMA((9,)),
        pltpu.SemaphoreType.DMA((9,)),
    ]
    smem = pl.BlockSpec(memory_space=pltpu.SMEM)
    whole = pl.BlockSpec(memory_space=pltpu.VMEM)
    hbm = pl.BlockSpec(memory_space=pl.ANY)
    sizes = (n_grp, n_row, n_col, fields, blocks, slots, coefs)
    out_b, out_f = pl.pallas_call(
        functools.partial(kernel, sizes),
        out_shape=[jax.ShapeDtypeStruct(right_side.shape, F32)] * 2,
        in_specs=[smem, smem, whole, whole, whole, whole, hbm, hbm, hbm, hbm, hbm],
        out_specs=[whole, whole],
        scratch_shapes=scratch,
        compiler_params=pltpu.CompilerParams(
            collective_id=0, has_side_effects=True, vmem_limit_bytes=60 << 20
        ),
    )(
        tile_pairs,
        tile_count,
        jnp.transpose(far_pick, (0, 2, 1)),
        leaf_of_panel,
        far_target,
        far_offset,
        right_side,
        near_tiles,
        exps,
        trans,
        tail,
    )
    return out_b + out_f


def solution(mesh):
    return jax.shard_map(
        local_part,
        mesh=mesh,
        in_specs=(
            P(None, None, "row"),
            P(None, ("grp", "row", "col"), None, None),
            P(("grp", "row", "col")),
            P(("grp", "row", "col")),
            P(None, "row", None),
            P("row", None),
            P(),
            P("row", None),
            P("row", None),
            P(),
        ),
        out_specs=P(None, None, "row"),
        check_vma=False,
    )
```
